256 devices in a mesh: row: 8 (over x, y_lo), col: 32 (over z, y_hi, core).
Axes of the slice: x: 4, y: 4 (y_hi: 2, y_lo: 2; y = y_hi * 2 + y_lo), z: 8, core: 2. Of those that a mesh axis runs over, the one named last changes fastest.
Arguments:
- prior_cov: float32 [4096, 4096], P('row', 'col'), as said below
- kernel: float32 [128, 2048], replicated, may hold values from -0.125 to 0.125
- offsets: int32 [128], replicated, may hold values from 0 to 2048
- obs_noise: float32 [128], replicated, may hold values from 64 to 512
- background: float32 [4096], P('col'), may hold values from -6 to 6
- observed: float32 [128], replicated, may hold values from -96 to 96
Outputs:
- analysis: float32 [4096], P('col')
- posterior: float32 [4096, 4096], P('row', 'col')
The draws below stay inside these ranges and needn't reach their ends.
Inputs may be any that keep to these rules, and one draw needn't show every extreme that they name: prior_cov is exactly symmetric and positive definite.
All inputs are finite; a program needn't handle non-finite values.
Results may differ from the reference program's by a relative error of at most 0.0003.
Values sent between devices are 32-bit elements; how exact they have to be, the bound alone decides.
A program may use at most 64 MiB of HBM per device.

```python
import math
import jax
import jax.numpy as jnp
from jax import lax

M = 128
N = 4096
KW = 2048


def draw_prior_cov(key, part):
    base_key = jax.random.fold_in(jax.random.fold_in(key, 17), 0)
    level_key = jax.random.fold_in(jax.random.fold_in(key, 17), 1)
    mode_key = jax.random.fold_in(jax.random.fold_in(key, 17), 3)
    freq_key, phase_key, amp_key = jax.random.split(mode_key, 3)
    mode_count = 64
    rough = jnp.clip(jax.random.normal(base_key, (N, N), jnp.float32), -6.0, 6.0)
    frequencies = jax.random.uniform(freq_key, (mode_count,), jnp.float32, 0.5, 8.0)
    phases = jax.random.uniform(phase_key, (mode_count,), jnp.float32, -3.1415927, 3.1415927)
    symmetric = (rough + rough.T) * 0.70710678
    amplitude = jax.random.uniform(amp_key, (mode_count,), jnp.float32, 0.5, 1.5) * math.sqrt(16.0 * math.sqrt(N) / mode_count)
    positions = jnp.arange(N, dtype=jnp.float32) / N
    modes = amplitude[None, :] * jnp.cos(6.2831853 * positions[:, None] * frequencies[None, :] + phases[None, :])
    smooth = jnp.dot(modes, modes.T, precision=lax.Precision.HIGHEST, preferred_element_type=jnp.float32)
    smooth = (smooth + smooth.T) * 0.5
    levels = jax.random.uniform(level_key, (N,), jnp.float32, 2.5, 4.0) * math.sqrt(N)
    diagonal_mask = jnp.arange(N)[:, None] == jnp.arange(N)[None, :]
    covariance = jnp.where(diagonal_mask, levels[:, None] + smooth, symmetric + smooth)
    return covariance


def with_ends(entries, rng, smallest, top_value):
    index_at = [jax.random.randint(jax.random.fold_in(rng, axis), (), 0, length) for axis, length in enumerate(entries.shape)]
    widest = entries.shape.index(max(entries.shape))
    neighbour = index_at[:widest] + [(index_at[widest] + 1) % entries.shape[widest]] + index_at[widest + 1:]
    return entries.at[tuple(index_at)].set(smallest).at[tuple(neighbour)].set(top_value)


def block_scale(key, shape, shards, low, high):
    def one(dim, shards_of):
        steps = jax.random.uniform(jax.random.fold_in(jax.random.fold_in(key, 6), dim), (shards_of,), jnp.float32, low / len(shards), high / len(shards))
        return jnp.repeat(jnp.exp(steps), shape[dim] // shards_of).reshape((-1,) + (1,) * (len(shape) - dim - 1))

    loudness = one(*shards[0])
    for cut in shards[1:]:
        loudness = loudness * one(*cut)
    return loudness


def noise(key, dims, deviation, bound, cuts=(), kind=jnp.bfloat16):
    result = jax.random.normal(key, dims, jnp.float32) * deviation
    if len(cuts) > 0:
        result = block_scale(key, dims, cuts, -0.22, 0.18) * result
    return jnp.clip(result, min=-bound, max=bound).astype(kind)


def setup_inputs(seed: int = 0) -> dict:
    key_of = jax.random.split(jax.random.key(seed), 7)
    prior_cov = draw_prior_cov(jax.random.fold_in(key_of[6], 71), 0)
    kernel = noise(key_of[1], (M, KW), KW ** -0.5, 0.125, (), jnp.float32)
    offsets = with_ends(jax.random.randint(key_of[2], (M,), 0, N - KW + 1), jax.random.fold_in(key_of[2], 1), 0, N - KW).astype(jnp.int32)
    obs_noise = jnp.clip(jnp.exp(jax.random.uniform(key_of[3], (M,), jnp.float32, math.log(64.0), math.log(512.0))), 64.0, 512.0)
    background = noise(key_of[4], (N,), 1.0, 6.0, ((0, 32),), jnp.float32)
    observed = noise(key_of[5], (M,), 16.0, 96.0, (), jnp.float32)
    return dict(prior_cov=prior_cov, kernel=kernel, offsets=offsets, obs_noise=obs_noise, background=background, observed=observed)


exact_mode = lax.Precision.HIGHEST

def build_operator(kernel, offsets, first_state, states):
    support = kernel.shape[1]
    position = first_state + jnp.arange(states, dtype=jnp.int32)[None, :] - offsets[:, None]
    inside = (position >= 0) & (position < support)
    picked = jnp.take_along_axis(kernel, jnp.clip(position, 0, support - 1).astype(jnp.int32), axis=1)
    return jnp.where(inside, picked, jnp.zeros_like(picked))

def reference(prior_cov, kernel, offsets, obs_noise, background, observed):
    operator = build_operator(kernel, offsets, 0, N)
    obs_image = jnp.dot(operator.astype(jnp.float32), prior_cov.astype(jnp.float32), precision=exact_mode, preferred_element_type=jnp.float32)
    innov_cov = lax.dot_general(obs_image.astype(jnp.float32), operator.astype(jnp.float32), (((1,), (1,)), ((), ())), precision=exact_mode, preferred_element_type=jnp.float32) + jnp.diag(obs_noise)
    innovation = observed - jnp.dot(operator.astype(jnp.float32), background.astype(jnp.float32), precision=exact_mode, preferred_element_type=jnp.float32)
    factor = jnp.linalg.cholesky(innov_cov)
    inverse = lax.linalg.triangular_solve(factor, jnp.eye(M, dtype=jnp.float32), left_side=True, lower=True)
    whitened = jnp.dot(inverse.astype(jnp.float32), obs_image.astype(jnp.float32), precision=exact_mode, preferred_element_type=jnp.float32)
    weights = jnp.dot(inverse.astype(jnp.float32), innovation.astype(jnp.float32), precision=exact_mode, preferred_element_type=jnp.float32)
    analysis = background + jnp.dot(weights.astype(jnp.float32), whitened.astype(jnp.float32), precision=exact_mode, preferred_element_type=jnp.float32)
    posterior = prior_cov - lax.dot_general(whitened.astype(jnp.float32), whitened.astype(jnp.float32), (((0,), (0,)), ((), ())), precision=exact_mode, preferred_element_type=jnp.float32)
    return (analysis, posterior)
```

```python
import jax
import jax.numpy as jnp
from jax import lax
from jax.experimental import pallas as pl
from jax.experimental.pallas import tpu as pltpu
from jax.sharding import PartitionSpec as P

MESH = pl.DeviceIdType.MESH
F32 = jnp.float32
BF16 = jnp.bfloat16
M = 128
LOW = 24
CHUNKS = 64
PIVOTS = 16


def mm(a, b):
    return jnp.dot(a, b, precision=lax.Precision.HIGHEST, preferred_element_type=F32)


def mm_nt(a, b):
    return lax.dot_general(
        a, b, (((1,), (1,)), ((), ())), precision=lax.Precision.HIGHEST, preferred_element_type=F32
    )


def split(a):
    high = a.astype(BF16)
    return high, (a - high.astype(F32)).astype(BF16)


def row_of(x, p):
    return jnp.broadcast_to(x[p : p + 1, :], x.shape)


def col_of(x, j):
    return jnp.broadcast_to(x[:, j : j + 1], x.shape)


def spd_inverse(blocks, b):
    count = M // b
    lane = lax.broadcasted_iota(jnp.int32, (b, M), 1)
    sub = lax.broadcasted_iota(jnp.int32, (b, M), 0)
    ahead = blocks[0]
    for k in range(count):
        inside = (lane >= k * b) & (lane < (k + 1) * b)
        cols = [col_of(ahead, k * b + j) for j in range(b)]
        top = jnp.where(inside, jnp.where(lane - k * b == sub, 1.0, 0.0), ahead)
        for p in range(b):
            scale = 1.0 / row_of(cols[p], p)
            is_p = sub == p
            t = row_of(top, p) * scale
            top = jnp.where(is_p, t, top - cols[p] * t)
            for j in range(p + 1, b):
                t = row_of(cols[j], p) * scale
                cols[j] = jnp.where(is_p, t, cols[j] - cols[p] * t)
        following = None
        if k + 1 < count:
            old = blocks[k + 1]
            following = jnp.where(inside, 0.0, old)
            for j in range(b):
                following = following - col_of(old, k * b + j) * row_of(top, j)
        if k + 1 < count or count > 1:
            a_hi, a_lo = split(jnp.concatenate(blocks, 0))
            t_hi, t_lo = split(top)

            def placed(t):
                parts = [t.astype(F32)]
                if k:
                    parts.insert(0, jnp.zeros((k * b, M), F32))
                if k + 1 < count:
                    parts.append(jnp.zeros((M - (k + 1) * b, M), F32))
                return jnp.concatenate(parts, 0).astype(BF16)

            t_hi, t_lo = placed(t_hi), placed(t_lo)
            update = (
                jnp.dot(a_hi, t_hi, preferred_element_type=F32)
                + jnp.dot(a_lo, t_hi, preferred_element_type=F32)
                + jnp.dot(a_hi, t_lo, preferred_element_type=F32)
            )
        new = []
        for i in range(count):
            if i == k:
                new.append(top)
            elif i == k + 1:
                new.append(following)
            else:
                new.append(jnp.where(inside, 0.0, blocks[i]) - update[i * b : (i + 1) * b])
        blocks, ahead = new, following
    return jnp.concatenate(blocks, 0)


def tree_sum(terms):
    while len(terms) > 1:
        terms = [sum(terms[i : i + 2][1:], terms[i]) for i in range(0, len(terms), 2)]
    return terms[0]


def kernel(
    prior_hbm, kernel_hbm, off_ref, noise_ref, bg_ref, obs_ref,
    ana_ref, post_hbm,
    kpad, hall, pv, outv,
    s_src, s_rs, z_src, z_rs, s_fin,
    m_src, m_rs, m2_src, m2_rs,
    g_src, g_rs, g_sl, g_col, g_row,
    load_sem, out_sem,
    s_send, s_recv, z_send, z_recv, f_send, f_recv,
    m_send, m_recv, m2_send, m2_recv, gs_send, gs_recv, gc_send, gc_recv, gr_send, gr_recv,
):
    r = lax.axis_index("row")
    c = lax.axis_index("col")
    z = c // 4
    y_hi = (c // 2) % 2
    core = c % 2
    q = r * 2 + y_hi
    w = z * 2 + core

    def plane(i):
        return (i // 2, z * 4 + (i % 2) * 2 + core)

    def column(i):
        return (r, (i // 2) * 4 + y_hi * 2 + i % 2)

    barrier = pltpu.get_barrier_semaphore()

    @pl.loop(1, 16)
    def _(i):
        pl.semaphore_signal(barrier, inc=1, device_id=plane((q + i) % 16), device_id_type=MESH)
        pl.semaphore_signal(barrier, inc=1, device_id=column((w + i) % 16), device_id_type=MESH)

    for k in range(16):
        pltpu.make_async_copy(
            kernel_hbm.at[:, pl.ds(k * 128, 128)], kpad.at[pl.ds((LOW + k) * 128, 128)], load_sem.at[0]
        ).start()
    prior_copy = pltpu.make_async_copy(prior_hbm, pv, load_sem.at[1])
    prior_copy.start()
    zeros = jnp.zeros((128, 128), F32)
    for start, stop in ((0, LOW), (LOW + 16, CHUNKS)):
        @pl.loop(start, stop)
        def _(i):
            kpad[pl.ds(pl.multiple_of(i * 128, 128), 128), :] = zeros

    data = kpad.at[pl.ds(LOW * 128, 16 * 128)]
    pltpu.make_async_copy(data, data, load_sem.at[0]).wait()

    lane = lax.broadcasted_iota(jnp.int32, (8, 128), 1)
    sub = lax.broadcasted_iota(jnp.int32, (8, 128), 0)

    def build(m, carry):
        off = off_ref[m]
        chunk = lax.shift_right_logical(off, 7)
        turn = lax.bitwise_and(off, 127)
        at_r = (LOW + 4 * r - chunk) * 128 + m
        at_c = (LOW + c - chunk) * 128 + m
        now = jnp.where(
            sub < 4, kpad[pl.ds(at_r, 8, stride=128), :], jnp.broadcast_to(kpad[pl.ds(at_c, 1), :], (8, 128))
        )
        before = jnp.where(
            sub < 4,
            kpad[pl.ds(at_r - 128, 8, stride=128), :],
            jnp.broadcast_to(kpad[pl.ds(at_c - 128, 1), :], (8, 128)),
        )
        turned = pltpu.roll(jnp.where(lane >= 128 - turn, before, now), turn, axis=1)
        hall[pl.ds(m, 8, stride=128), :] = turned
        return carry

    lax.fori_loop(0, M, build, 0, unroll=8)

    prior_copy.wait()
    part = mm(hall[0:128, :], pv[0:128, :])
    for j in range(1, 4):
        part += mm(hall[j * 128 : (j + 1) * 128, :], pv[j * 128 : (j + 1) * 128, :])
    h_c = hall[512:640, :]
    s_part = mm_nt(h_c, part)
    s_src[...] = s_part.reshape(16, 8, 128)
    s_rs[q] = s_src[q]

    pl.semaphore_wait(barrier, 30)

    @pl.loop(1, 16)
    def _(i):
        to = (q + i) % 16
        pltpu.make_async_remote_copy(
            s_src.at[to], s_rs.at[q], s_send, s_recv, device_id=plane(to), device_id_type=MESH
        ).start()

    g_src[...] = jnp.transpose(part).reshape(8, 16, 128)
    g_rs[r] = g_src[r]

    @pl.loop(1, 8)
    def _(i):
        to = (r + i) % 8
        pltpu.make_async_remote_copy(
            g_src.at[to], g_rs.at[r], gs_send, gs_recv, device_id=(to, c), device_id_type=MESH
        ).start()

    bg8 = jnp.broadcast_to(bg_ref[...], (8, 128))
    mean = mm_nt(bg8, h_c)
    m_src[0] = mean
    m_rs[w] = mean

    @pl.loop(1, 16)
    def _(i):
        pltpu.make_async_remote_copy(
            m_src.at[0], m_rs.at[w], m_send, m_recv, device_id=column((w + i) % 16), device_id_type=MESH
        ).start()

    def arrived(buffer, count, send, recv):
        view = buffer.at[pl.ds(0, count)]
        return pltpu.make_async_remote_copy(view, view, send, recv, device_id=(r, c), device_id_type=MESH)

    arrived(s_rs, 15, s_send, s_recv).wait_recv()
    tile = tree_sum([s_rs[i] for i in range(16)])
    z_src[0] = tile
    z_rs[w] = tile

    @pl.loop(1, 16)
    def _(i):
        pltpu.make_async_remote_copy(
            z_src.at[0], z_rs.at[w], z_send, z_recv, device_id=column((w + i) % 16), device_id_type=MESH
        ).start()

    arrived(g_rs, 7, gs_send, gs_recv).wait_recv()
    g_sl[0] = tree_sum([g_rs[i] for i in range(8)])

    arrived(m_rs, 15, m_send, m_recv).wait_recv()
    mean = tree_sum([m_rs[i] for i in range(16)])
    m2_src[0] = mean

    arrived(z_rs, 15, z_send, z_recv).wait_recv()
    tile = tree_sum([z_rs[i] for i in range(16)])
    s_fin[q] = tile
    z_src[1] = tile

    @pl.loop(1, 16)
    def _(i):
        pltpu.make_async_remote_copy(
            z_src.at[1], s_fin.at[q], f_send, f_recv, device_id=plane((q + i) % 16), device_id_type=MESH
        ).start()

    other = r * 2 + 1 - y_hi
    mean_copy = pltpu.make_async_remote_copy(
        m2_src, m2_rs, m2_send, m2_recv, device_id=plane(other), device_id_type=MESH
    )
    mean_copy.start()

    arrived(s_fin, 15, f_send, f_recv).wait_recv()

    @pl.loop(1, 8)
    def _(i):
        pltpu.make_async_remote_copy(
            g_sl.at[0], g_col.at[r], gc_send, gc_recv, device_id=((r + i) % 8, c), device_id_type=MESH
        ).start()

    slot = (c % 4) * 8 + r

    @pl.loop(1, 32)
    def _(i):
        pltpu.make_async_remote_copy(
            g_sl.at[0], g_row.at[slot], gr_send, gr_recv, device_id=(z, (c + i) % 32), device_id_type=MESH
        ).start()

    @pl.when(z == r)
    def _():
        pltpu.make_async_copy(g_sl.at[0], g_row.at[slot], gr_recv).start()

    @pl.when(z != r)
    def _():
        pltpu.make_async_remote_copy(
            g_sl.at[0], g_row.at[slot], gr_send, gr_recv, device_id=(z, c), device_id_type=MESH
        ).start()

    g_col[r] = g_sl[0]

    s_all = s_fin[...].reshape(128, 128)
    rows = lax.broadcasted_iota(jnp.int32, (128, 128), 0)
    lanes = lax.broadcasted_iota(jnp.int32, (128, 128), 1)
    s_all = s_all + jnp.where(rows == lanes, jnp.broadcast_to(noise_ref[...], (128, 128)), 0.0)
    inverse = spd_inverse([s_all[i * PIVOTS : (i + 1) * PIVOTS] for i in range(M // PIVOTS)], PIVOTS)

    arrived(g_col, 7, gc_send, gc_recv).wait_recv()
    solved = mm(g_col[...].reshape(128, 128), inverse)

    mean_copy.wait_recv()
    mean = m2_src[0] + m2_rs[0]
    innovation = jnp.broadcast_to(obs_ref[...], (8, 128)) - mean
    ana_ref[...] = bg_ref[...] + mm_nt(innovation, solved)[0:1, :]

    arrived(g_row, 32, gr_send, gr_recv).wait_recv()
    for j in range(4):
        g_j = g_row[j * 8 : (j + 1) * 8].reshape(128, 128)
        outv[j] = pv[j * 128 : (j + 1) * 128, :] - mm_nt(g_j, solved)
        pltpu.make_async_copy(outv.at[j], post_hbm.at[pl.ds(j * 128, 128)], out_sem.at[j]).start()

    arrived(s_rs, 15, s_send, s_recv).wait_send()
    arrived(z_rs, 15, z_send, z_recv).wait_send()
    arrived(s_fin, 15, f_send, f_recv).wait_send()
    arrived(m_rs, 15, m_send, m_recv).wait_send()
    arrived(g_rs, 7, gs_send, gs_recv).wait_send()
    arrived(g_col, 7, gc_send, gc_recv).wait_send()
    mean_copy.wait_send()

    @pl.when(z == r)
    def _():
        arrived(g_row, 31, gr_send, gr_recv).wait_send()

    @pl.when(z != r)
    def _():
        arrived(g_row, 32, gr_send, gr_recv).wait_send()

    for j in range(4):
        pltpu.make_async_copy(outv.at[j], post_hbm.at[pl.ds(j * 128, 128)], out_sem.at[j]).wait()


def on_device(prior_cov, kern, offsets, obs_noise, background, observed):
    vmem = pl.BlockSpec(memory_space=pltpu.VMEM)
    hbm = pl.BlockSpec(memory_space=pl.ANY)
    dma = pltpu.SemaphoreType.DMA
    ana, post = pl.pallas_call(
        kernel,
        name="analysis",
        out_shape=(jax.ShapeDtypeStruct((1, 128), F32), jax.ShapeDtypeStruct((512, 128), F32)),
        in_specs=[hbm, hbm, pl.BlockSpec(memory_space=pltpu.SMEM), vmem, vmem, vmem],
        out_specs=(vmem, hbm),
        scratch_shapes=[
            pltpu.VMEM((CHUNKS * 128, 128), F32),
            pltpu.VMEM((8 * 128, 128), F32),
            pltpu.VMEM((512, 128), F32),
            pltpu.VMEM((4, 128, 128), F32),
            pltpu.VMEM((16, 8, 128), F32),
            pltpu.VMEM((16, 8, 128), F32),
            pltpu.VMEM((2, 8, 128), F32),
            pltpu.VMEM((16, 8, 128), F32),
            pltpu.VMEM((16, 8, 128), F32),
            pltpu.VMEM((1, 8, 128), F32),
            pltpu.VMEM((16, 8, 128), F32),
            pltpu.VMEM((1, 8, 128), F32),
            pltpu.VMEM((1, 8, 128), F32),
            pltpu.VMEM((8, 16, 128), F32),
            pltpu.VMEM((8, 16, 128), F32),
            pltpu.VMEM((1, 16, 128), F32),
            pltpu.VMEM((8, 16, 128), F32),
            pltpu.VMEM((32, 16, 128), F32),
            dma((2,)),
            dma((4,)),
        ]
        + [dma] * 16,
        compiler_params=pltpu.CompilerParams(
            collective_id=0, has_side_effects=True, vmem_limit_bytes=32 * 1024 * 1024
        ),
    )(
        prior_cov,
        kern,
        offsets,
        obs_noise.reshape(1, 128),
        background.reshape(1, 128),
        observed.reshape(1, 128),
    )
    return ana.reshape(128), post


def solution(mesh):
    placed = (P("row", "col"), P(), P(), P(), P("col"), P())
    return jax.shard_map(
        on_device,
        mesh=mesh,
        in_specs=placed,
        out_specs=(P("col"), P("row", "col")),
        check_vma=False,
    )
```

```python
import jax
import jax.numpy as jnp
from jax import lax
from jax.experimental import pallas as pl
from jax.experimental.pallas import tpu as pltpu
from jax.sharding import PartitionSpec as P

MESH = pl.DeviceIdType.MESH
F32 = jnp.float32
M = 128
LOW = 24
CHUNKS = 64
STRIDE = 136
GROUP = 32
PIVOTS = 16


def mm(a, b):
    return jnp.dot(a, b, precision=lax.Precision.HIGHEST, preferred_element_type=F32)


def mm_nt(a, b):
    return lax.dot_general(
        a, b, (((1,), (1,)), ((), ())), precision=lax.Precision.HIGHEST, preferred_element_type=F32
    )


def row_of(x, p):
    return jnp.broadcast_to(x[p : p + 1, :], x.shape)


def col_of(x, j):
    return jnp.broadcast_to(x[:, j : j + 1], x.shape)


def spd_inverse(blocks, b):
    count = M // b
    lane = lax.broadcasted_iota(jnp.int32, (b, M), 1)
    sub = lax.broadcasted_iota(jnp.int32, (b, M), 0)
    ahead = blocks[0]
    for k in range(count):
        inside = (lane >= k * b) & (lane < (k + 1) * b)
        cols = [col_of(ahead, k * b + j) for j in range(b)]
        top = jnp.where(inside, jnp.where(lane - k * b == sub, 1.0, 0.0), ahead)
        for p in range(b):
            scale = 1.0 / row_of(cols[p], p)
            is_p = sub == p
            t = row_of(top, p) * scale
            top = jnp.where(is_p, t, top - cols[p] * t)
            for j in range(p + 1, b):
                t = row_of(cols[j], p) * scale
                cols[j] = jnp.where(is_p, t, cols[j] - cols[p] * t)
        following = None
        if k + 1 < count:
            old = blocks[k + 1]
            following = jnp.where(inside, 0.0, old)
            for j in range(b):
                following = following - col_of(old, k * b + j) * row_of(top, j)
        parts = [top]
        if k:
            parts.insert(0, jnp.zeros((k * b, M), F32))
        if k + 1 < count:
            parts.append(jnp.zeros((M - (k + 1) * b, M), F32))
        update = mm(jnp.concatenate(blocks, 0), jnp.concatenate(parts, 0))
        new = []
        for i in range(count):
            if i == k:
                new.append(top)
            elif i == k + 1:
                new.append(following)
            else:
                new.append(jnp.where(inside, 0.0, blocks[i]) - update[i * b : (i + 1) * b])
        blocks, ahead = new, following
    return jnp.concatenate(blocks, 0)


def tree_sum(terms):
    while len(terms) > 1:
        terms = [sum(terms[i : i + 2][1:], terms[i]) for i in range(0, len(terms), 2)]
    return terms[0]


def kernel(
    prior_hbm, kernel_hbm, off_hbm, noise_hbm, bg_hbm, obs_hbm,
    ana_ref, post_ref,
    off_ref, vec, kpad, hall, pv,
    s_src, s_rs, z_src, z_rs, s_fin, m_src, m_rs, g_src, g_rs, g_sl, g_col, g_row,
    load_sem,
    s_send, s_recv, z_send, z_recv, f_send, f_recv, m_send, m_recv,
    gs_send, gs_recv, gc_send, gc_recv, gr_send, gr_recv, sb_send, sb_recv,
):
    r = lax.axis_index("row")
    c = lax.axis_index("col")
    z = c // 4
    y_hi = (c // 2) % 2
    core = c % 2
    q = r * 2 + y_hi
    p = q * 2 + core
    owner = core == y_hi

    def plane(i):
        return (i // 4, z * 4 + i % 4)

    def summer(tile):
        return (tile // 2, z * 4 + (tile % 2) * 3)

    def send(source, target, send_sem, recv_sem, device):
        pltpu.make_async_remote_copy(
            source, target, send_sem, recv_sem, device_id=device, device_id_type=MESH
        ).start()

    def total(buffer, count, send_sem, recv_sem):
        view = buffer.at[pl.ds(0, count)]
        return pltpu.make_async_remote_copy(
            view, view, send_sem, recv_sem, device_id=(r, c), device_id_type=MESH
        )

    barrier = pltpu.get_barrier_semaphore()

    off_copy = pltpu.make_async_copy(off_hbm, off_ref, load_sem.at[0])
    off_copy.start()
    for k in range(16):
        pltpu.make_async_copy(
            kernel_hbm.at[:, pl.ds(k * 128, 128)], kpad.at[LOW + k, pl.ds(0, 128)], load_sem.at[1]
        ).start()
    prior_copy = pltpu.make_async_copy(prior_hbm, pv, load_sem.at[2])
    prior_copy.start()
    vec_copies = [
        pltpu.make_async_copy(source, vec.at[i], load_sem.at[3 + i])
        for i, source in enumerate((noise_hbm, bg_hbm, obs_hbm))
    ]
    for copy in vec_copies:
        copy.start()

    @pl.loop(1, 32)
    def _(i):
        pl.semaphore_signal(barrier, inc=1, device_id=plane((p + i) % 32), device_id_type=MESH)
        pl.semaphore_signal(barrier, inc=1, device_id=(r, (c + i) % 32), device_id_type=MESH)

    zeros = jnp.zeros((STRIDE, 128), F32)
    for start, stop in ((0, LOW), (LOW + 16, CHUNKS)):
        @pl.loop(start, stop)
        def _(i):
            kpad[i] = zeros

    off_copy.wait()
    data = kpad.at[pl.ds(LOW, 16), pl.ds(0, 128)]
    pltpu.make_async_copy(data, data, load_sem.at[1]).wait()

    lane = lax.broadcasted_iota(jnp.int32, (8, 128), 1)
    sub = lax.broadcasted_iota(jnp.int32, (8, 128), 0)
    flat = kpad.reshape(CHUNKS * STRIDE, 128)

    def build(group, carry):
        built = []
        for u in range(GROUP):
            m = group * GROUP + u
            off = off_ref[m]
            chunk = lax.shift_right_logical(off, 7)
            turn = lax.bitwise_and(off, 127)
            at_r = (LOW + 4 * r - chunk) * STRIDE + m
            at_c = (LOW + c - chunk) * STRIDE + m
            now = jnp.where(
                sub < 4, flat[pl.ds(at_r, 8, stride=STRIDE), :], flat[pl.ds(at_c, 8, stride=0), :]
            )
            before = jnp.where(
                sub < 4,
                flat[pl.ds(at_r - STRIDE, 8, stride=STRIDE), :],
                flat[pl.ds(at_c - STRIDE, 8, stride=0), :],
            )
            turned = pltpu.roll(jnp.where(lane >= 128 - turn, before, now), turn, axis=1)
            built.append((m, turned))
        for m, turned in built:
            hall[pl.ds(m, 8, stride=STRIDE), :] = turned
        return carry

    lax.fori_loop(0, M // GROUP, build, 0)

    prior_copy.wait()
    part = mm(hall[0:128, :], pv[0:128, :])
    for j in range(1, 4):
        part += mm(hall[j * STRIDE : j * STRIDE + 128, :], pv[j * 128 : (j + 1) * 128, :])
    h_c = hall[4 * STRIDE : 4 * STRIDE + 128, :]
    s_src[...] = mm_nt(h_c, part).reshape(16, 8, 128)

    pl.semaphore_wait(barrier, 62)

    @pl.loop(1, 16)
    def _(i):
        to = (q + i) % 16
        send(s_src.at[to], s_rs.at[p], s_send, s_recv, summer(to))

    @pl.when(owner)
    def _():
        s_rs[p] = s_src[q]

    @pl.when(jnp.logical_not(owner))
    def _():
        send(s_src.at[q], s_rs.at[p], s_send, s_recv, summer(q))

    g_src[...] = jnp.transpose(part).reshape(8, 16, 128)
    g_rs[r] = g_src[r]

    @pl.loop(1, 8)
    def _(i):
        to = (r + i) % 8
        send(g_src.at[to], g_rs.at[r], gs_send, gs_recv, (to, c))

    for copy in vec_copies:
        copy.wait()
    mean = mm_nt(jnp.broadcast_to(vec[1], (8, 128)), h_c)[0:1, :]
    m_src[0] = mean
    m_rs[c] = mean

    @pl.loop(1, 32)
    def _(i):
        send(m_src.at[0], m_rs.at[c], m_send, m_recv, (r, (c + i) % 32))

    @pl.when(owner)
    def _():
        total(s_rs, 31, s_send, s_recv).wait_recv()
        tile = tree_sum([s_rs[i] for i in range(32)])
        z_src[0] = tile
        z_rs[z] = tile

        @pl.loop(1, 8)
        def _(i):
            send(z_src.at[0], z_rs.at[z], z_send, z_recv, (r, (c + 4 * i) % 32))

    total(g_rs, 7, gs_send, gs_recv).wait_recv()
    g_sl[0] = tree_sum([g_rs[i] for i in range(8)])
    slot = core * 16 + y_hi * 8 + r

    @pl.loop(1, 16)
    def _(i):
        to = (z * 2 + y_hi + i) % 16
        send(g_sl.at[0], g_row.at[slot], gr_send, gr_recv, (z, (to // 2) * 4 + (to % 2) * 2 + core))

    @pl.when(z == r)
    def _():
        pltpu.make_async_copy(g_sl.at[0], g_row.at[slot], gr_recv).start()

    @pl.when(z != r)
    def _():
        send(g_sl.at[0], g_row.at[slot], gr_send, gr_recv, (z, c))

    g_col[r] = g_sl[0]

    @pl.loop(1, 8)
    def _(i):
        send(g_sl.at[0], g_col.at[r], gc_send, gc_recv, ((r + i) % 8, c))

    @pl.when(owner)
    def _():
        total(z_rs, 7, z_send, z_recv).wait_recv()
        tile = tree_sum([z_rs[i] for i in range(8)])
        z_src[1] = tile
        s_fin[q] = tile

        @pl.loop(1, 32)
        def _(i):
            send(z_src.at[1], s_fin.at[q], f_send, f_recv, plane((p + i) % 32))

    total(g_row, 16, gr_send, gr_recv).wait_recv()
    half = g_row.at[pl.ds(core * 16, 16)]
    share = pltpu.make_async_remote_copy(
        half, half, sb_send, sb_recv, device_id=(r, c + 1 - 2 * core), device_id_type=MESH
    )
    share.start()

    @pl.when(owner)
    def _():
        total(s_fin, 15, f_send, f_recv).wait_recv()

    @pl.when(jnp.logical_not(owner))
    def _():
        total(s_fin, 16, f_send, f_recv).wait_recv()

    rows = lax.broadcasted_iota(jnp.int32, (128, 128), 0)
    lanes = lax.broadcasted_iota(jnp.int32, (128, 128), 1)
    noise = jnp.where(rows == lanes, jnp.broadcast_to(vec[0], (128, 128)), 0.0)
    s_all = s_fin[...].reshape(128, 128) + noise
    inverse = spd_inverse([s_all[i * PIVOTS : (i + 1) * PIVOTS] for i in range(M // PIVOTS)], PIVOTS)

    total(g_col, 7, gc_send, gc_recv).wait_recv()
    solved = mm(g_col[...].reshape(128, 128), inverse)

    share.wait_recv()
    for j in range(4):
        first = (j % 2) * 16 + (j // 2) * 8
        g_j = g_row[first : first + 8].reshape(128, 128)
        here = slice(j * 128, (j + 1) * 128)
        post_ref[here, :] = pv[here, :] - mm_nt(g_j, solved)

    total(m_rs, 31, m_send, m_recv).wait_recv()
    mean = tree_sum([m_rs[i] for i in range(32)])
    innovation = jnp.broadcast_to(vec[2] - mean, (8, 128))
    ana_ref[...] = vec[1] + mm_nt(innovation, solved)[0:1, :]

    @pl.when(owner)
    def _():
        total(s_rs, 15, s_send, s_recv).wait_send()
        total(z_rs, 7, z_send, z_recv).wait_send()
        total(s_rs, 31, f_send, f_recv).wait_send()

    @pl.when(jnp.logical_not(owner))
    def _():
        total(s_rs, 16, s_send, s_recv).wait_send()

    total(m_rs, 31, m_send, m_recv).wait_send()
    total(g_rs, 7, gs_send, gs_recv).wait_send()
    total(g_col, 7, gc_send, gc_recv).wait_send()
    share.wait_send()

    @pl.when(z == r)
    def _():
        total(g_row, 15, gr_send, gr_recv).wait_send()

    @pl.when(z != r)
    def _():
        total(g_row, 16, gr_send, gr_recv).wait_send()


def on_device(prior_cov, kern, offsets, obs_noise, background, observed):
    vmem = pl.BlockSpec(memory_space=pltpu.VMEM)
    hbm = pl.BlockSpec(memory_space=pltpu.HBM)
    dma = pltpu.SemaphoreType.DMA

    def tiles(count, rows=8):
        return pltpu.VMEM((count, rows, 128), F32)

    ana, post = pl.pallas_call(
        kernel,
        name="analysis",
        out_shape=(jax.ShapeDtypeStruct((1, 128), F32), jax.ShapeDtypeStruct((512, 128), F32)),
        in_specs=[hbm] * 6,
        out_specs=(vmem, vmem),
        scratch_shapes=[
            pltpu.SMEM((128,), jnp.int32),
            tiles(3, 1),
            tiles(CHUNKS, STRIDE),
            pltpu.VMEM((8 * STRIDE, 128), F32),
            pltpu.VMEM((512, 128), F32),
            tiles(16), tiles(32), tiles(2), tiles(8), tiles(16),
            tiles(1, 1), tiles(32, 1),
            tiles(8, 16), tiles(8, 16), tiles(1, 16), tiles(8, 16), tiles(32, 16),
            dma((6,)),
        ]
        + [dma] * 16,
        compiler_params=pltpu.CompilerParams(
            collective_id=0, has_side_effects=True, vmem_limit_bytes=66519040
        ),
    )(
        prior_cov,
        kern,
        offsets,
        obs_noise.reshape(1, 128),
        background.reshape(1, 128),
        observed.reshape(1, 128),
    )
    return ana.reshape(128), post


def solution(mesh):
    placed = (P("row", "col"), P(), P(), P(), P("col"), P())
    return jax.shard_map(
        on_device,
        mesh=mesh,
        in_specs=placed,
        out_specs=(P("col"), P("row", "col")),
        check_vma=False,
    )
```

```python
import jax
import jax.numpy as jnp
from jax import lax
from jax.experimental import pallas as pl
from jax.experimental.pallas import tpu as pltpu
from jax.sharding import PartitionSpec as P

MESH = pl.DeviceIdType.MESH
F32 = jnp.float32
M = 128
LOW = 24
CHUNKS = 64
STRIDE = 136
GROUP = 32
PIVOTS = 16


def mm(a, b):
    return jnp.dot(a, b, precision=lax.Precision.HIGHEST, preferred_element_type=F32)


def mm_nt(a, b):
    return lax.dot_general(
        a, b, (((1,), (1,)), ((), ())), precision=lax.Precision.HIGHEST, preferred_element_type=F32
    )


def row_of(x, p):
    return jnp.broadcast_to(x[p : p + 1, :], x.shape)


def col_of(x, j):
    return jnp.broadcast_to(x[:, j : j + 1], x.shape)


def spd_inverse(blocks, b):
    count = M // b
    lane = lax.broadcasted_iota(jnp.int32, (b, M), 1)
    sub = lax.broadcasted_iota(jnp.int32, (b, M), 0)
    ahead = blocks[0]
    for k in range(count):
        inside = (lane >= k * b) & (lane < (k + 1) * b)
        cols = [col_of(ahead, k * b + j) for j in range(b)]
        top = jnp.where(inside, jnp.where(lane - k * b == sub, 1.0, 0.0), ahead)
        for p in range(b):
            scale = 1.0 / row_of(cols[p], p)
            is_p = sub == p
            t = row_of(top, p) * scale
            top = jnp.where(is_p, t, top - cols[p] * t)
            for j in range(p + 1, b):
                t = row_of(cols[j], p) * scale
                cols[j] = jnp.where(is_p, t, cols[j] - cols[p] * t)
        following = None
        if k + 1 < count:
            old = blocks[k + 1]
            following = jnp.where(inside, 0.0, old)
            for j in range(b):
                following = following - col_of(old, k * b + j) * row_of(top, j)
        parts = [top]
        if k:
            parts.insert(0, jnp.zeros((k * b, M), F32))
        if k + 1 < count:
            parts.append(jnp.zeros((M - (k + 1) * b, M), F32))
        update = mm(jnp.concatenate(blocks, 0), jnp.concatenate(parts, 0))
        new = []
        for i in range(count):
            if i == k:
                new.append(top)
            elif i == k + 1:
                new.append(following)
            else:
                new.append(jnp.where(inside, 0.0, blocks[i]) - update[i * b : (i + 1) * b])
        blocks, ahead = new, following
    return jnp.concatenate(blocks, 0)


def tree_sum(terms):
    while len(terms) > 1:
        terms = [sum(terms[i : i + 2][1:], terms[i]) for i in range(0, len(terms), 2)]
    return terms[0]


def kernel(
    prior_hbm, kernel_hbm, off_hbm, noise_hbm, bg_hbm, obs_hbm,
    solved_ref, innovation_ref, pv, g_row,
    off_ref, vec, kpad, hall,
    s_src, s_rs, z_src, z_rs, s_fin, m_src, m_rs, g_src, g_rs, g_sl, g_col,
    load_sem,
    s_send, s_recv, z_send, z_recv, f_send, f_recv, m_send, m_recv,
    gs_send, gs_recv, gc_send, gc_recv, gr_send, gr_recv, sb_send, sb_recv,
):
    r = lax.axis_index("row")
    c = lax.axis_index("col")
    z = c // 4
    y_hi = (c // 2) % 2
    core = c % 2
    q = r * 2 + y_hi
    p = q * 2 + core
    owner = core == y_hi

    def plane(i):
        return (i // 4, z * 4 + i % 4)

    def summer(tile):
        return (tile // 2, z * 4 + (tile % 2) * 3)

    def send(source, target, send_sem, recv_sem, device):
        pltpu.make_async_remote_copy(
            source, target, send_sem, recv_sem, device_id=device, device_id_type=MESH
        ).start()

    def total(buffer, count, send_sem, recv_sem):
        view = buffer.at[pl.ds(0, count)]
        return pltpu.make_async_remote_copy(
            view, view, send_sem, recv_sem, device_id=(r, c), device_id_type=MESH
        )

    barrier = pltpu.get_barrier_semaphore()

    off_copy = pltpu.make_async_copy(off_hbm, off_ref, load_sem.at[0])
    off_copy.start()
    for k in range(16):
        pltpu.make_async_copy(
            kernel_hbm.at[:, pl.ds(k * 128, 128)], kpad.at[LOW + k, pl.ds(0, 128)], load_sem.at[1]
        ).start()
    prior_copy = pltpu.make_async_copy(prior_hbm, pv, load_sem.at[2])
    prior_copy.start()
    vec_copies = [
        pltpu.make_async_copy(source, vec.at[i], load_sem.at[3 + i])
        for i, source in enumerate((noise_hbm, bg_hbm, obs_hbm))
    ]
    for copy in vec_copies:
        copy.start()

    @pl.loop(1, 32)
    def _(i):
        pl.semaphore_signal(barrier, inc=1, device_id=plane((p + i) % 32), device_id_type=MESH)
        pl.semaphore_signal(barrier, inc=1, device_id=(r, (c + i) % 32), device_id_type=MESH)

    zeros = jnp.zeros((STRIDE, 128), F32)
    for start, stop in ((0, LOW), (LOW + 16, CHUNKS)):
        @pl.loop(start, stop)
        def _(i):
            kpad[i] = zeros

    off_copy.wait()
    data = kpad.at[pl.ds(LOW, 16), pl.ds(0, 128)]
    pltpu.make_async_copy(data, data, load_sem.at[1]).wait()

    lane = lax.broadcasted_iota(jnp.int32, (8, 128), 1)
    sub = lax.broadcasted_iota(jnp.int32, (8, 128), 0)
    flat = kpad.reshape(CHUNKS * STRIDE, 128)

    def build(group, carry):
        built = []
        for u in range(GROUP):
            m = group * GROUP + u
            off = off_ref[m]
            chunk = lax.shift_right_logical(off, 7)
            turn = lax.bitwise_and(off, 127)
            at_r = (LOW + 4 * r - chunk) * STRIDE + m
            at_c = (LOW + c - chunk) * STRIDE + m
            now = jnp.where(
                sub < 4, flat[pl.ds(at_r, 8, stride=STRIDE), :], flat[pl.ds(at_c, 8, stride=0), :]
            )
            before = jnp.where(
                sub < 4,
                flat[pl.ds(at_r - STRIDE, 8, stride=STRIDE), :],
                flat[pl.ds(at_c - STRIDE, 8, stride=0), :],
            )
            turned = pltpu.roll(jnp.where(lane >= 128 - turn, before, now), turn, axis=1)
            built.append((m, turned))
        for m, turned in built:
            hall[pl.ds(m, 8, stride=STRIDE), :] = turned
        return carry

    lax.fori_loop(0, M // GROUP, build, 0)

    prior_copy.wait()
    part = mm(hall[0:128, :], pv[0:128, :])
    for j in range(1, 4):
        part += mm(hall[j * STRIDE : j * STRIDE + 128, :], pv[j * 128 : (j + 1) * 128, :])
    h_c = hall[4 * STRIDE : 4 * STRIDE + 128, :]
    s_src[...] = mm_nt(h_c, part).reshape(16, 8, 128)

    pl.semaphore_wait(barrier, 62)

    @pl.loop(1, 16)
    def _(i):
        to = (q + i) % 16
        send(s_src.at[to], s_rs.at[p], s_send, s_recv, summer(to))

    @pl.when(owner)
    def _():
        s_rs[p] = s_src[q]

    @pl.when(jnp.logical_not(owner))
    def _():
        send(s_src.at[q], s_rs.at[p], s_send, s_recv, summer(q))

    g_src[...] = jnp.transpose(part).reshape(8, 16, 128)
    g_rs[r] = g_src[r]

    @pl.loop(1, 8)
    def _(i):
        to = (r + i) % 8
        send(g_src.at[to], g_rs.at[r], gs_send, gs_recv, (to, c))

    for copy in vec_copies:
        copy.wait()
    mean = mm_nt(jnp.broadcast_to(vec[1], (8, 128)), h_c)[0:1, :]
    m_src[0] = mean
    m_rs[c] = mean

    @pl.loop(1, 32)
    def _(i):
        send(m_src.at[0], m_rs.at[c], m_send, m_recv, (r, (c + i) % 32))

    @pl.when(owner)
    def _():
        total(s_rs, 31, s_send, s_recv).wait_recv()
        tile = tree_sum([s_rs[i] for i in range(32)])
        z_src[0] = tile
        z_rs[z] = tile

        @pl.loop(1, 8)
        def _(i):
            send(z_src.at[0], z_rs.at[z], z_send, z_recv, (r, (c + 4 * i) % 32))

    total(g_rs, 7, gs_send, gs_recv).wait_recv()
    g_sl[0] = tree_sum([g_rs[i] for i in range(8)])
    slot = core * 16 + y_hi * 8 + r

    @pl.loop(1, 16)
    def _(i):
        to = (z * 2 + y_hi + i) % 16
        send(g_sl.at[0], g_row.at[slot], gr_send, gr_recv, (z, (to // 2) * 4 + (to % 2) * 2 + core))

    @pl.when(z == r)
    def _():
        pltpu.make_async_copy(g_sl.at[0], g_row.at[slot], gr_recv).start()

    @pl.when(z != r)
    def _():
        send(g_sl.at[0], g_row.at[slot], gr_send, gr_recv, (z, c))

    g_col[r] = g_sl[0]

    @pl.loop(1, 8)
    def _(i):
        send(g_sl.at[0], g_col.at[r], gc_send, gc_recv, ((r + i) % 8, c))

    @pl.when(owner)
    def _():
        total(z_rs, 7, z_send, z_recv).wait_recv()
        tile = tree_sum([z_rs[i] for i in range(8)])
        z_src[1] = tile
        s_fin[q] = tile

        @pl.loop(1, 32)
        def _(i):
            send(z_src.at[1], s_fin.at[q], f_send, f_recv, plane((p + i) % 32))

    total(g_row, 16, gr_send, gr_recv).wait_recv()
    half = g_row.at[pl.ds(core * 16, 16)]
    share = pltpu.make_async_remote_copy(
        half, half, sb_send, sb_recv, device_id=(r, c + 1 - 2 * core), device_id_type=MESH
    )
    share.start()

    @pl.when(owner)
    def _():
        total(s_fin, 15, f_send, f_recv).wait_recv()

    @pl.when(jnp.logical_not(owner))
    def _():
        total(s_fin, 16, f_send, f_recv).wait_recv()

    rows = lax.broadcasted_iota(jnp.int32, (128, 128), 0)
    lanes = lax.broadcasted_iota(jnp.int32, (128, 128), 1)
    noise = jnp.where(rows == lanes, jnp.broadcast_to(vec[0], (128, 128)), 0.0)
    s_all = s_fin[...].reshape(128, 128) + noise
    inverse = spd_inverse([s_all[i * PIVOTS : (i + 1) * PIVOTS] for i in range(M // PIVOTS)], PIVOTS)

    total(m_rs, 31, m_send, m_recv).wait_recv()
    mean = tree_sum([m_rs[i] for i in range(32)])
    innovation_ref[...] = jnp.broadcast_to(vec[2] - mean, (8, 128))

    total(g_col, 7, gc_send, gc_recv).wait_recv()
    solved_ref[...] = mm(g_col[...].reshape(128, 128), inverse)

    share.wait_recv()

    @pl.when(owner)
    def _():
        total(s_rs, 15, s_send, s_recv).wait_send()
        total(z_rs, 7, z_send, z_recv).wait_send()
        total(s_rs, 31, f_send, f_recv).wait_send()

    @pl.when(jnp.logical_not(owner))
    def _():
        total(s_rs, 16, s_send, s_recv).wait_send()

    total(m_rs, 31, m_send, m_recv).wait_send()
    total(g_rs, 7, gs_send, gs_recv).wait_send()
    total(g_col, 7, gc_send, gc_recv).wait_send()
    share.wait_send()

    @pl.when(z == r)
    def _():
        total(g_row, 15, gr_send, gr_recv).wait_send()

    @pl.when(z != r)
    def _():
        total(g_row, 16, gr_send, gr_recv).wait_send()


def finish(solved_ref, innovation_ref, pv, g_row, bg_hbm, ana_hbm, post_hbm, bg, ana, post, sem):
    bg_copy = pltpu.make_async_copy(bg_hbm, bg, sem.at[0])
    bg_copy.start()
    solved = solved_ref[...]
    copies = []
    for j in range(4):
        first = (j % 2) * 16 + (j // 2) * 8
        g_j = g_row[first : first + 8].reshape(128, 128)
        here = slice(j * 128, (j + 1) * 128)
        post[here, :] = pv[here, :] - mm_nt(g_j, solved)
        copies.append(pltpu.make_async_copy(post.at[here], post_hbm.at[here], sem.at[1 + j]))
        copies[-1].start()
    bg_copy.wait()
    ana[...] = bg[...] + mm_nt(innovation_ref[...], solved)[0:1, :]
    copies.append(pltpu.make_async_copy(ana, ana_hbm, sem.at[5]))
    copies[-1].start()
    for copy in copies:
        copy.wait()


def on_device(prior_cov, kern, offsets, obs_noise, background, observed):
    vmem = pl.BlockSpec(memory_space=pltpu.VMEM)
    hbm = pl.BlockSpec(memory_space=pltpu.HBM)
    dma = pltpu.SemaphoreType.DMA

    def tiles(count, rows=8):
        return pltpu.VMEM((count, rows, 128), F32)

    def array(*shape):
        return jax.ShapeDtypeStruct(shape, F32)

    operands = [
        pltpu.with_memory_space_constraint(x, pltpu.HBM)
        for x in (
            prior_cov,
            kern,
            offsets,
            obs_noise.reshape(1, 128),
            background.reshape(1, 128),
            observed.reshape(1, 128),
        )
    ]
    solved, innovation, prior_copy, pieces = pl.pallas_call(
        kernel,
        name="analysis",
        out_shape=(array(128, 128), array(8, 128), array(512, 128), array(32, 16, 128)),
        in_specs=[hbm] * 6,
        out_specs=(vmem,) * 4,
        scratch_shapes=[
            pltpu.SMEM((128,), jnp.int32),
            tiles(3, 1),
            tiles(CHUNKS, STRIDE),
            pltpu.VMEM((8 * STRIDE, 128), F32),
            tiles(16), tiles(32), tiles(2), tiles(8), tiles(16),
            tiles(1, 1), tiles(32, 1),
            tiles(8, 16), tiles(8, 16), tiles(1, 16), tiles(8, 16),
            dma((6,)),
        ]
        + [dma] * 16,
        compiler_params=pltpu.CompilerParams(
            collective_id=0, has_side_effects=True, vmem_limit_bytes=40 * 1024 * 1024
        ),
    )(*operands)
    ana, post = pl.pallas_call(
        finish,
        name="finish",
        out_shape=(array(1, 128), array(512, 128)),
        in_specs=[vmem] * 4 + [hbm],
        out_specs=(hbm, hbm),
        scratch_shapes=[
            pltpu.VMEM((1, 128), F32), pltpu.VMEM((1, 128), F32), pltpu.VMEM((512, 128), F32), dma((6,)),
        ],
        compiler_params=pltpu.CompilerParams(vmem_limit_bytes=40 * 1024 * 1024),
    )(solved, innovation, prior_copy, pieces, operands[4])
    return ana.reshape(128), post


def solution(mesh):
    placed = (P("row", "col"), P(), P(), P(), P("col"), P())
    return jax.shard_map(
        on_device,
        mesh=mesh,
        in_specs=placed,
        out_specs=(P("col"), P("row", "col")),
        check_vma=False,
    )
```

```python
import jax
import jax.numpy as jnp
from jax import lax
from jax.experimental import pallas as pl
from jax.experimental.pallas import tpu as pltpu
from jax.sharding import PartitionSpec as P

MESH = pl.DeviceIdType.MESH
F32 = jnp.float32
M = 128
LOW = 24
CHUNKS = 64
STRIDE = 136
GROUP = 64
GAP = GROUP + 8


def ring(d, n):
    return min(d, n - d)


PLANE_STEPS = sorted(
    ((dx, dy) for dx in range(4) for dy in range(4) if dx or dy), key=lambda d: -ring(d[0], 4) - ring(d[1], 4)
)
PLANES_STEPS = sorted(range(1, 8), key=lambda d: -ring(d, 8))
PIVOTS = 16


def mm(a, b):
    return jnp.dot(a, b, precision=lax.Precision.HIGHEST, preferred_element_type=F32)


def mm_nt(a, b):
    return lax.dot_general(
        a, b, (((1,), (1,)), ((), ())), precision=lax.Precision.HIGHEST, preferred_element_type=F32
    )


def row_of(x, p):
    return jnp.broadcast_to(x[p : p + 1, :], x.shape)


def col_of(x, j):
    return jnp.broadcast_to(x[:, j : j + 1], x.shape)


def spd_inverse(blocks, b):
    count = M // b
    lane = lax.broadcasted_iota(jnp.int32, (b, M), 1)
    sub = lax.broadcasted_iota(jnp.int32, (b, M), 0)
    ahead = blocks[0]
    for k in range(count):
        inside = (lane >= k * b) & (lane < (k + 1) * b)
        cols = [col_of(ahead, k * b + j) for j in range(b)]
        top = jnp.where(inside, jnp.where(lane - k * b == sub, 1.0, 0.0), ahead)
        for p in range(b):
            scale = 1.0 / row_of(cols[p], p)
            is_p = sub == p
            t = row_of(top, p) * scale
            top = jnp.where(is_p, t, top - cols[p] * t)
            for j in range(p + 1, b):
                t = row_of(cols[j], p) * scale
                cols[j] = jnp.where(is_p, t, cols[j] - cols[p] * t)
        following = None
        if k + 1 < count:
            old = blocks[k + 1]
            following = jnp.where(inside, 0.0, old)
            for j in range(b):
                following = following - col_of(old, k * b + j) * row_of(top, j)
        parts = [top]
        if k:
            parts.insert(0, jnp.zeros((k * b, M), F32))
        if k + 1 < count:
            parts.append(jnp.zeros((M - (k + 1) * b, M), F32))
        update = mm(jnp.concatenate(blocks, 0), jnp.concatenate(parts, 0))
        new = []
        for i in range(count):
            if i == k:
                new.append(top)
            elif i == k + 1:
                new.append(following)
            else:
                new.append(jnp.where(inside, 0.0, blocks[i]) - update[i * b : (i + 1) * b])
        blocks, ahead = new, following
    return jnp.concatenate(blocks, 0)


def tree_sum(terms):
    while len(terms) > 1:
        terms = [sum(terms[i : i + 2][1:], terms[i]) for i in range(0, len(terms), 2)]
    return terms[0]


def kernel(
    prior_hbm, kernel_hbm, off_hbm, noise_hbm, bg_hbm, obs_hbm,
    solved_ref, innovation_ref, pv, g_row,
    off_ref, vec, kpad_0, kpad_1, hall,
    s_src, s_rs, z_src, z_rs, s_fin, m_src, m_rs, m_all, g_src, g_rs, g_sl, g_col,
    load_sem, group_sem, ready,
    s_send, s_recv, z_send, z_recv, f_send, f_recv, m_send, m_recv, ma_send, ma_recv,
    gs_send, gs_recv, gc_send, gc_recv, gr_send, gr_recv, sb_send, sb_recv,
):
    r = lax.axis_index("row")
    c = lax.axis_index("col")
    z = c // 4
    y_hi = (c // 2) % 2
    core = c % 2
    q = r * 2 + y_hi
    p = q * 2 + core
    owner = core == y_hi

    x = r // 2
    y = y_hi * 2 + r % 2

    def chip(dx, dy):
        to_x, to_y = (x + dx) % 4, (y + dy) % 4
        return to_x * 2 + to_y % 2, to_y // 2

    def plane(i):
        return (i // 4, z * 4 + i % 4)

    def send(source, target, send_sem, recv_sem, device):
        pltpu.make_async_remote_copy(
            source, target, send_sem, recv_sem, device_id=device, device_id_type=MESH
        ).start()

    def total(buffer, count, send_sem, recv_sem):
        view = buffer.at[pl.ds(0, count)]
        return pltpu.make_async_remote_copy(
            view, view, send_sem, recv_sem, device_id=(r, c), device_id_type=MESH
        )

    barrier = pltpu.get_barrier_semaphore()

    def greet(device):
        pl.semaphore_signal(barrier, inc=1, device_id=device, device_id_type=MESH)

    for dx, dy in PLANE_STEPS:
        row, half = chip(dx, dy)
        greet((row, z * 4 + half * 2))
        greet((row, z * 4 + half * 2 + 1))
    for dz in PLANES_STEPS:
        greet((r, (c + 4 * dz) % 32))
    greet((r, c + 1 - 2 * core))

    off_copy = pltpu.make_async_copy(off_hbm, off_ref, load_sem.at[0])
    off_copy.start()
    kpads = (kpad_0, kpad_1)
    for group in range(M // GROUP):
        rows = pl.ds(group * GROUP, GROUP)
        for k in range(16):
            pltpu.make_async_copy(
                kernel_hbm.at[rows, pl.ds(k * 128, 128)], kpads[group].at[LOW + k, pl.ds(0, GROUP)], group_sem.at[group]
            ).start()
    prior_copy = pltpu.make_async_copy(prior_hbm, pv, load_sem.at[2])
    prior_copy.start()
    vec_copies = [
        pltpu.make_async_copy(source, vec.at[i], load_sem.at[3 + i])
        for i, source in enumerate((noise_hbm, bg_hbm, obs_hbm))
    ]
    for copy in vec_copies:
        copy.start()

    zeros = jnp.zeros((GROUP, 128), F32)
    for start, stop in ((LOW - 17, LOW), (LOW + 16, LOW + 32)):
        @pl.loop(start, stop)
        def _(i):
            for kpad in kpads:
                kpad[i, 0:GROUP] = zeros

    off_copy.wait()

    lane = lax.broadcasted_iota(jnp.int32, (8, 128), 1)
    sub = lax.broadcasted_iota(jnp.int32, (8, 128), 0)

    for group in range(M // GROUP):
        data = kpads[group].at[pl.ds(LOW, 16), pl.ds(0, GROUP)]
        flat = kpads[group].reshape(CHUNKS * GAP, 128)
        pltpu.make_async_copy(data, data, group_sem.at[group]).wait()
        built = []
        for u in range(GROUP):
            m = group * GROUP + u
            off = off_ref[m]
            chunk = lax.shift_right_logical(off, 7)
            turn = lax.bitwise_and(off, 127)
            at_r = (LOW + 4 * r - chunk) * GAP + u
            at_c = (LOW + c - chunk) * GAP + u
            now = jnp.where(
                sub < 4, flat[pl.ds(at_r, 8, stride=GAP), :], flat[pl.ds(at_c, 8, stride=0), :]
            )
            before = jnp.where(
                sub < 4,
                flat[pl.ds(at_r - GAP, 8, stride=GAP), :],
                flat[pl.ds(at_c - GAP, 8, stride=0), :],
            )
            turned = pltpu.roll(jnp.where(lane >= 128 - turn, before, now), turn, axis=1)
            built.append((m, turned))
        for m, turned in built:
            hall[pl.ds(m, 8, stride=STRIDE), :] = turned

    prior_copy.wait()
    h_r = jnp.concatenate([hall[j * STRIDE : j * STRIDE + 128, :] for j in range(4)], 1)
    part = mm(h_r, pv[...])
    h_c = hall[4 * STRIDE : 4 * STRIDE + 128, :]
    s_src[...] = mm_nt(h_c, part).reshape(16, 8, 128)

    pl.semaphore_wait(barrier, 38)

    for dx, dy in PLANE_STEPS:
        row, half = chip(dx, dy)
        to = row * 2 + half
        send(s_src.at[to], s_rs.at[p], s_send, s_recv, (row, z * 4 + half * 3))

    @pl.when(owner)
    def _():
        s_rs[p] = s_src[q]

    @pl.when(jnp.logical_not(owner))
    def _():
        send(s_src.at[q], s_rs.at[p], s_send, s_recv, (r, z * 4 + y_hi * 3))

    g_src[...] = jnp.transpose(part).reshape(8, 16, 128)
    g_rs[r] = g_src[r]

    @pl.loop(1, 8)
    def _(i):
        to = (r + i) % 8
        send(g_src.at[to], g_rs.at[r], gs_send, gs_recv, (to, c))

    for copy in vec_copies:
        copy.wait()
    mean = mm_nt(jnp.broadcast_to(vec[1], (8, 128)), h_c)[0:1, :]
    m_src[0] = mean
    m_rs[z] = mean

    @pl.loop(1, 8)
    def _(i):
        send(m_src.at[0], m_rs.at[z], m_send, m_recv, (r, (c + 4 * i) % 32))

    @pl.loop(0, 8)
    def _(i):
        pl.semaphore_signal(
            ready, inc=1, device_id=(i, z * 4 + (1 - y_hi) * 2 + core), device_id_type=MESH
        )

    @pl.when(owner)
    def _():
        total(s_rs, 31, s_send, s_recv).wait_recv()
        tile = tree_sum([s_rs[i] for i in range(32)])
        z_src[0] = tile
        z_rs[z] = tile
        for dz in PLANES_STEPS:
            send(z_src.at[0], z_rs.at[z], z_send, z_recv, (r, (c + 4 * dz) % 32))

    total(g_rs, 7, gs_send, gs_recv).wait_recv()
    pl.semaphore_wait(ready, 8)
    piece = tree_sum([g_rs[i] for i in range(8)])
    g_sl[0] = piece
    g_col[r] = piece
    slot = core * 16 + y_hi * 8 + r

    @pl.loop(1, 16)
    def _(i):
        to = (z * 2 + y_hi + i) % 16
        send(g_sl.at[0], g_row.at[slot], gr_send, gr_recv, (z, (to // 2) * 4 + (to % 2) * 2 + core))

    @pl.when(z == r)
    def _():
        pltpu.make_async_copy(g_sl.at[0], g_row.at[slot], gr_recv).start()

    @pl.when(z != r)
    def _():
        send(g_sl.at[0], g_row.at[slot], gr_send, gr_recv, (z, c))

    @pl.loop(1, 8)
    def _(i):
        send(g_sl.at[0], g_col.at[r], gc_send, gc_recv, ((r + i) % 8, c))

    @pl.when(owner)
    def _():
        total(z_rs, 7, z_send, z_recv).wait_recv()
        tile = tree_sum([z_rs[i] for i in range(8)])
        z_src[1] = tile
        s_fin[q] = tile

        for dx, dy in PLANE_STEPS + [(0, 0)]:
            row, half = chip(dx, dy)
            for other in (0, 1):
                if dx or dy:
                    to = (row, z * 4 + half * 2 + other)
                elif other:
                    to = (r, c + 1 - 2 * core)
                else:
                    continue
                send(z_src.at[1], s_fin.at[q], f_send, f_recv, to)

    total(m_rs, 7, m_send, m_recv).wait_recv()
    m_src[1] = tree_sum([m_rs[i] for i in range(8)])
    place = y_hi * 2 + core
    m_all[place] = m_src[1]

    @pl.loop(1, 4)
    def _(i):
        send(m_src.at[1], m_all.at[place], ma_send, ma_recv, (r, z * 4 + (place + i) % 4))

    total(g_row, 16, gr_send, gr_recv).wait_recv()
    half = g_row.at[pl.ds(core * 16, 16)]
    share = pltpu.make_async_remote_copy(
        half, half, sb_send, sb_recv, device_id=(r, c + 1 - 2 * core), device_id_type=MESH
    )
    share.start()

    @pl.when(owner)
    def _():
        total(s_fin, 15, f_send, f_recv).wait_recv()

    @pl.when(jnp.logical_not(owner))
    def _():
        total(s_fin, 16, f_send, f_recv).wait_recv()

    rows = lax.broadcasted_iota(jnp.int32, (128, 128), 0)
    lanes = lax.broadcasted_iota(jnp.int32, (128, 128), 1)
    noise = jnp.where(rows == lanes, jnp.broadcast_to(vec[0], (128, 128)), 0.0)
    s_all = s_fin[...].reshape(128, 128) + noise
    inverse = spd_inverse([s_all[i * PIVOTS : (i + 1) * PIVOTS] for i in range(M // PIVOTS)], PIVOTS)

    total(m_all, 3, ma_send, ma_recv).wait_recv()
    mean = tree_sum([m_all[i] for i in range(4)])
    innovation_ref[...] = jnp.broadcast_to(vec[2] - mean, (8, 128))

    total(g_col, 7, gc_send, gc_recv).wait_recv()
    solved_ref[...] = mm(g_col[...].reshape(128, 128), inverse)

    share.wait_recv()

    @pl.when(owner)
    def _():
        total(s_rs, 15, s_send, s_recv).wait_send()
        total(z_rs, 7, z_send, z_recv).wait_send()
        total(s_rs, 31, f_send, f_recv).wait_send()

    @pl.when(jnp.logical_not(owner))
    def _():
        total(s_rs, 16, s_send, s_recv).wait_send()

    total(m_rs, 7, m_send, m_recv).wait_send()
    total(m_all, 3, ma_send, ma_recv).wait_send()
    total(g_rs, 7, gs_send, gs_recv).wait_send()
    total(g_col, 7, gc_send, gc_recv).wait_send()
    share.wait_send()

    @pl.when(z == r)
    def _():
        total(g_row, 15, gr_send, gr_recv).wait_send()

    @pl.when(z != r)
    def _():
        total(g_row, 16, gr_send, gr_recv).wait_send()


def finish(solved_ref, innovation_ref, pv, g_row, bg_hbm, ana_hbm, post_hbm, bg, ana, post, sem):
    bg_copy = pltpu.make_async_copy(bg_hbm, bg, sem.at[0])
    bg_copy.start()
    solved = solved_ref[...]
    copies = []
    for j in range(4):
        first = (j % 2) * 16 + (j // 2) * 8
        g_j = g_row[first : first + 8].reshape(128, 128)
        here = slice(j * 128, (j + 1) * 128)
        post[here, :] = pv[here, :] - mm_nt(g_j, solved)
        copies.append(pltpu.make_async_copy(post.at[here], post_hbm.at[here], sem.at[1 + j]))
        copies[-1].start()
    bg_copy.wait()
    ana[...] = bg[...] + mm_nt(innovation_ref[...], solved)[0:1, :]
    copies.append(pltpu.make_async_copy(ana, ana_hbm, sem.at[5]))
    copies[-1].start()
    for copy in copies:
        copy.wait()


def on_device(prior_cov, kern, offsets, obs_noise, background, observed):
    vmem = pl.BlockSpec(memory_space=pltpu.VMEM)
    hbm = pl.BlockSpec(memory_space=pltpu.HBM)
    dma = pltpu.SemaphoreType.DMA

    def tiles(count, rows=8):
        return pltpu.VMEM((count, rows, 128), F32)

    def array(*shape):
        return jax.ShapeDtypeStruct(shape, F32)

    operands = [
        pltpu.with_memory_space_constraint(x, pltpu.HBM)
        for x in (
            prior_cov,
            kern,
            offsets,
            obs_noise.reshape(1, 128),
            background.reshape(1, 128),
            observed.reshape(1, 128),
        )
    ]
    solved, innovation, prior_copy, pieces = pl.pallas_call(
        kernel,
        name="analysis",
        out_shape=(array(128, 128), array(8, 128), array(512, 128), array(32, 16, 128)),
        in_specs=[hbm] * 6,
        out_specs=(vmem,) * 4,
        scratch_shapes=[
            pltpu.SMEM((128,), jnp.int32),
            tiles(3, 1),
            tiles(CHUNKS, GAP),
            tiles(CHUNKS, GAP),
            pltpu.VMEM((8 * STRIDE, 128), F32),
            tiles(16), tiles(32), tiles(2), tiles(8), tiles(16),
            tiles(2, 1), tiles(8, 1), tiles(4, 1),
            tiles(8, 16), tiles(8, 16), tiles(1, 16), tiles(8, 16),
            dma((6,)),
            dma((M // GROUP,)),
            pltpu.SemaphoreType.REGULAR,
        ]
        + [dma] * 18,
        compiler_params=pltpu.CompilerParams(
            collective_id=0, has_side_effects=True, vmem_limit_bytes=40 * 1024 * 1024
        ),
    )(*operands)
    ana, post = pl.pallas_call(
        finish,
        name="finish",
        out_shape=(array(1, 128), array(512, 128)),
        in_specs=[vmem] * 4 + [hbm],
        out_specs=(hbm, hbm),
        scratch_shapes=[
            pltpu.VMEM((1, 128), F32), pltpu.VMEM((1, 128), F32), pltpu.VMEM((512, 128), F32), dma((6,)),
        ],
        compiler_params=pltpu.CompilerParams(vmem_limit_bytes=40 * 1024 * 1024),
    )(solved, innovation, prior_copy, pieces, operands[4])
    return ana.reshape(128), post


def solution(mesh):
    placed = (P("row", "col"), P(), P(), P(), P("col"), P())
    return jax.shard_map(
        on_device,
        mesh=mesh,
        in_specs=placed,
        out_specs=(P("col"), P("row", "col")),
        check_vma=False,
    )
```

```python
import jax
import jax.numpy as jnp
from jax import lax
from jax.experimental import pallas as pl
from jax.experimental.pallas import tpu as pltpu
from jax.sharding import PartitionSpec as P

MESH = pl.DeviceIdType.MESH
F32 = jnp.float32
M = 128
LOW = 24
CHUNKS = 64
STRIDE = 136
GROUP = 64
GAP = GROUP + 8


def ring(d, n):
    return min(d, n - d)


PLANE_STEPS = sorted(
    ((dx, dy) for dx in range(4) for dy in range(4) if dx or dy), key=lambda d: -ring(d[0], 4) - ring(d[1], 4)
)
PLANES_STEPS = sorted(range(1, 8), key=lambda d: -ring(d, 8))
PIVOTS = 16


def mm(a, b):
    return jnp.dot(a, b, precision=lax.Precision.HIGHEST, preferred_element_type=F32)


def mm_nt(a, b):
    return lax.dot_general(
        a, b, (((1,), (1,)), ((), ())), precision=lax.Precision.HIGHEST, preferred_element_type=F32
    )


def row_of(x, p):
    return jnp.broadcast_to(x[p : p + 1, :], x.shape)


def col_of(x, j):
    return jnp.broadcast_to(x[:, j : j + 1], x.shape)


def spd_inverse(blocks, b):
    count = M // b
    lane = lax.broadcasted_iota(jnp.int32, (b, M), 1)
    sub = lax.broadcasted_iota(jnp.int32, (b, M), 0)
    ahead = blocks[0]
    for k in range(count):
        inside = (lane >= k * b) & (lane < (k + 1) * b)
        cols = [col_of(ahead, k * b + j) for j in range(b)]
        top = jnp.where(inside, jnp.where(lane - k * b == sub, 1.0, 0.0), ahead)
        for p in range(b):
            scale = 1.0 / row_of(cols[p], p)
            is_p = sub == p
            t = row_of(top, p) * scale
            top = jnp.where(is_p, t, top - cols[p] * t)
            for j in range(p + 1, b):
                t = row_of(cols[j], p) * scale
                cols[j] = jnp.where(is_p, t, cols[j] - cols[p] * t)
        following = None
        if k + 1 < count:
            old = blocks[k + 1]
            following = jnp.where(inside, 0.0, old)
            for j in range(b):
                following = following - col_of(old, k * b + j) * row_of(top, j)
        parts = [top]
        if k:
            parts.insert(0, jnp.zeros((k * b, M), F32))
        if k + 1 < count:
            parts.append(jnp.zeros((M - (k + 1) * b, M), F32))
        update = mm(jnp.concatenate(blocks, 0), jnp.concatenate(parts, 0))
        new = []
        for i in range(count):
            if i == k:
                new.append(top)
            elif i == k + 1:
                new.append(following)
            else:
                new.append(jnp.where(inside, 0.0, blocks[i]) - update[i * b : (i + 1) * b])
        blocks, ahead = new, following
    return jnp.concatenate(blocks, 0)


def tree_sum(terms):
    while len(terms) > 1:
        terms = [sum(terms[i : i + 2][1:], terms[i]) for i in range(0, len(terms), 2)]
    return terms[0]


def kernel(
    prior_hbm, kernel_hbm, off_hbm, noise_hbm, bg_hbm, obs_hbm,
    solved_ref, vectors_ref, pv, g_row,
    off_ref, vec, kpad_0, kpad_1, hall,
    s_src, s_rs, z_src, z_rs, s_fin, m_src, m_rs, m_all, g_src, g_rs, g_sl, g_col,
    load_sem, group_sem, ready,
    s_send, s_recv, z_send, z_recv, f_send, f_recv, m_send, m_recv, ma_send, ma_recv,
    gs_send, gs_recv, gc_send, gc_recv, gr_send, gr_recv, sb_send, sb_recv,
):
    r = lax.axis_index("row")
    c = lax.axis_index("col")
    z = c // 4
    y_hi = (c // 2) % 2
    core = c % 2
    q = r * 2 + y_hi
    p = q * 2 + core
    owner = core == y_hi

    x = r // 2
    y = y_hi * 2 + r % 2

    def chip(dx, dy):
        to_x, to_y = (x + dx) % 4, (y + dy) % 4
        return to_x * 2 + to_y % 2, to_y // 2

    def plane(i):
        return (i // 4, z * 4 + i % 4)

    def send(source, target, send_sem, recv_sem, device):
        pltpu.make_async_remote_copy(
            source, target, send_sem, recv_sem, device_id=device, device_id_type=MESH
        ).start()

    def total(buffer, count, send_sem, recv_sem):
        view = buffer.at[pl.ds(0, count)]
        return pltpu.make_async_remote_copy(
            view, view, send_sem, recv_sem, device_id=(r, c), device_id_type=MESH
        )

    barrier = pltpu.get_barrier_semaphore()

    def greet(device):
        pl.semaphore_signal(barrier, inc=1, device_id=device, device_id_type=MESH)

    greetings = [(ring(dz, 8) + 0.5, (r, (c + 4 * dz) % 32)) for dz in range(1, 8)]
    for dx, dy in PLANE_STEPS:
        row, half = chip(dx, dy)
        for other in (0, 1):
            greetings.append((ring(dx, 4) + ring(dy, 4), (row, z * 4 + half * 2 + other)))
    greetings.sort(key=lambda g: -g[0])
    greetings = [device for _, device in greetings] + [(r, c + 1 - 2 * core)]
    for device in greetings[:16]:
        greet(device)

    off_copy = pltpu.make_async_copy(off_hbm, off_ref, load_sem.at[0])
    off_copy.start()
    kpads = (kpad_0, kpad_1)
    for group in range(M // GROUP):
        rows = pl.ds(group * GROUP, GROUP)
        for k in range(16):
            pltpu.make_async_copy(
                kernel_hbm.at[rows, pl.ds(k * 128, 128)], kpads[group].at[LOW + k, pl.ds(0, GROUP)], group_sem.at[group]
            ).start()
        if group == 0:
            for device in greetings[16:]:
                greet(device)
    prior_copy = pltpu.make_async_copy(prior_hbm, pv, load_sem.at[2])
    prior_copy.start()
    vec_copies = [
        pltpu.make_async_copy(source, vec.at[i], load_sem.at[3 + i])
        for i, source in enumerate((noise_hbm, bg_hbm, obs_hbm))
    ]
    for copy in vec_copies:
        copy.start()

    zeros = jnp.zeros((GROUP, 128), F32)
    for start, stop in ((LOW - 17, LOW), (LOW + 16, LOW + 32)):
        @pl.loop(start, stop)
        def _(i):
            for kpad in kpads:
                kpad[i, 0:GROUP] = zeros

    off_copy.wait()

    lane = lax.broadcasted_iota(jnp.int32, (8, 128), 1)
    sub = lax.broadcasted_iota(jnp.int32, (8, 128), 0)

    for group in range(M // GROUP):
        data = kpads[group].at[pl.ds(LOW, 16), pl.ds(0, GROUP)]
        flat = kpads[group].reshape(CHUNKS * GAP, 128)
        pltpu.make_async_copy(data, data, group_sem.at[group]).wait()
        built = []
        for u in range(GROUP):
            m = group * GROUP + u
            off = off_ref[m]
            chunk = lax.shift_right_logical(off, 7)
            turn = lax.bitwise_and(off, 127)
            at_r = (LOW + 4 * r - chunk) * GAP + u
            at_c = (LOW + c - chunk) * GAP + u
            now = jnp.where(
                sub < 4, flat[pl.ds(at_r, 8, stride=GAP), :], flat[pl.ds(at_c, 8, stride=0), :]
            )
            before = jnp.where(
                sub < 4,
                flat[pl.ds(at_r - GAP, 8, stride=GAP), :],
                flat[pl.ds(at_c - GAP, 8, stride=0), :],
            )
            turned = pltpu.roll(jnp.where(lane >= 128 - turn, before, now), turn, axis=1)
            built.append((m, turned))
        for m, turned in built:
            hall[pl.ds(m, 8, stride=STRIDE), :] = turned

    prior_copy.wait()
    h_r = jnp.concatenate([hall[j * STRIDE : j * STRIDE + 128, :] for j in range(4)], 1)
    part = mm(h_r, pv[...])
    h_c = hall[4 * STRIDE : 4 * STRIDE + 128, :]
    s_src[...] = mm_nt(h_c, part).reshape(16, 8, 128)

    pl.semaphore_wait(barrier, 38)

    for dx, dy in PLANE_STEPS:
        row, half = chip(dx, dy)
        to = row * 2 + half
        send(s_src.at[to], s_rs.at[p], s_send, s_recv, (row, z * 4 + half * 3))

    @pl.when(owner)
    def _():
        s_rs[p] = s_src[q]

    @pl.when(jnp.logical_not(owner))
    def _():
        send(s_src.at[q], s_rs.at[p], s_send, s_recv, (r, z * 4 + y_hi * 3))

    g_src[...] = jnp.transpose(part).reshape(8, 16, 128)
    g_rs[r] = g_src[r]

    @pl.loop(1, 8)
    def _(i):
        to = (r + i) % 8
        send(g_src.at[to], g_rs.at[r], gs_send, gs_recv, (to, c))

    for copy in vec_copies:
        copy.wait()
    mean = mm_nt(jnp.broadcast_to(vec[1], (8, 128)), h_c)[0:1, :]
    m_src[0] = mean
    m_rs[z] = mean

    @pl.loop(1, 8)
    def _(i):
        send(m_src.at[0], m_rs.at[z], m_send, m_recv, (r, (c + 4 * i) % 32))

    @pl.loop(0, 8)
    def _(i):
        pl.semaphore_signal(
            ready, inc=1, device_id=(i, z * 4 + (1 - y_hi) * 2 + core), device_id_type=MESH
        )

    @pl.when(owner)
    def _():
        total(s_rs, 31, s_send, s_recv).wait_recv()
        tile = tree_sum([s_rs[i] for i in range(32)])
        z_src[0] = tile
        z_rs[z] = tile
        for dz in PLANES_STEPS:
            send(z_src.at[0], z_rs.at[z], z_send, z_recv, (r, (c + 4 * dz) % 32))

    total(g_rs, 7, gs_send, gs_recv).wait_recv()
    pl.semaphore_wait(ready, 8)
    piece = tree_sum([g_rs[i] for i in range(8)])
    g_sl[0] = piece
    g_col[r] = piece
    slot = core * 16 + y_hi * 8 + r

    @pl.loop(1, 16)
    def _(i):
        to = (z * 2 + y_hi + i) % 16
        send(g_sl.at[0], g_row.at[slot], gr_send, gr_recv, (z, (to // 2) * 4 + (to % 2) * 2 + core))

    @pl.when(z == r)
    def _():
        pltpu.make_async_copy(g_sl.at[0], g_row.at[slot], gr_recv).start()

    @pl.when(z != r)
    def _():
        send(g_sl.at[0], g_row.at[slot], gr_send, gr_recv, (z, c))

    @pl.loop(1, 8)
    def _(i):
        send(g_sl.at[0], g_col.at[r], gc_send, gc_recv, ((r + i) % 8, c))

    @pl.when(owner)
    def _():
        total(z_rs, 7, z_send, z_recv).wait_recv()
        tile = tree_sum([z_rs[i] for i in range(8)])
        z_src[1] = tile
        s_fin[q] = tile

        for dx, dy in PLANE_STEPS + [(0, 0)]:
            row, half = chip(dx, dy)
            for other in (0, 1):
                if dx or dy:
                    to = (row, z * 4 + half * 2 + other)
                elif other:
                    to = (r, c + 1 - 2 * core)
                else:
                    continue
                send(z_src.at[1], s_fin.at[q], f_send, f_recv, to)

    total(m_rs, 7, m_send, m_recv).wait_recv()
    m_src[1] = tree_sum([m_rs[i] for i in range(8)])
    place = y_hi * 2 + core
    m_all[place] = m_src[1]

    @pl.loop(1, 4)
    def _(i):
        send(m_src.at[1], m_all.at[place], ma_send, ma_recv, (r, z * 4 + (place + i) % 4))

    total(g_row, 16, gr_send, gr_recv).wait_recv()
    half = g_row.at[pl.ds(core * 16, 16)]
    share = pltpu.make_async_remote_copy(
        half, half, sb_send, sb_recv, device_id=(r, c + 1 - 2 * core), device_id_type=MESH
    )
    share.start()

    @pl.when(owner)
    def _():
        total(s_fin, 15, f_send, f_recv).wait_recv()

    @pl.when(jnp.logical_not(owner))
    def _():
        total(s_fin, 16, f_send, f_recv).wait_recv()

    rows = lax.broadcasted_iota(jnp.int32, (128, 128), 0)
    lanes = lax.broadcasted_iota(jnp.int32, (128, 128), 1)
    noise = jnp.where(rows == lanes, jnp.broadcast_to(vec[0], (128, 128)), 0.0)
    s_all = s_fin[...].reshape(128, 128) + noise
    inverse = spd_inverse([s_all[i * PIVOTS : (i + 1) * PIVOTS] for i in range(M // PIVOTS)], PIVOTS)

    total(m_all, 3, ma_send, ma_recv).wait_recv()
    mean = tree_sum([m_all[i] for i in range(4)])
    vectors_ref[0] = jnp.broadcast_to(vec[2] - mean, (8, 128))
    vectors_ref[1] = jnp.broadcast_to(vec[1], (8, 128))

    total(g_col, 7, gc_send, gc_recv).wait_recv()
    solved_ref[...] = mm(g_col[...].reshape(128, 128), inverse)

    share.wait_recv()

    @pl.when(owner)
    def _():
        total(s_rs, 15, s_send, s_recv).wait_send()
        total(z_rs, 7, z_send, z_recv).wait_send()
        total(s_rs, 31, f_send, f_recv).wait_send()

    @pl.when(jnp.logical_not(owner))
    def _():
        total(s_rs, 16, s_send, s_recv).wait_send()

    total(m_rs, 7, m_send, m_recv).wait_send()
    total(m_all, 3, ma_send, ma_recv).wait_send()
    total(g_rs, 7, gs_send, gs_recv).wait_send()
    total(g_col, 7, gc_send, gc_recv).wait_send()
    share.wait_send()

    @pl.when(z == r)
    def _():
        total(g_row, 15, gr_send, gr_recv).wait_send()

    @pl.when(z != r)
    def _():
        total(g_row, 16, gr_send, gr_recv).wait_send()


def finish(solved_ref, vectors_ref, pv, g_row, ana_hbm, post_hbm, ana, post, sem):
    solved = solved_ref[...]
    ana[...] = (vectors_ref[1] + mm_nt(vectors_ref[0], solved))[0:1, :]
    copies = [pltpu.make_async_copy(ana, ana_hbm, sem.at[4])]
    copies[0].start()
    for j in range(4):
        first = (j % 2) * 16 + (j // 2) * 8
        g_j = g_row[first : first + 8].reshape(128, 128)
        here = slice(j * 128, (j + 1) * 128)
        post[here, :] = pv[here, :] - mm_nt(g_j, solved)
        copies.append(pltpu.make_async_copy(post.at[here], post_hbm.at[here], sem.at[j]))
        copies[-1].start()
    for copy in copies:
        copy.wait()


def on_device(prior_cov, kern, offsets, obs_noise, background, observed):
    vmem = pl.BlockSpec(memory_space=pltpu.VMEM)
    hbm = pl.BlockSpec(memory_space=pltpu.HBM)
    dma = pltpu.SemaphoreType.DMA

    def tiles(count, rows=8):
        return pltpu.VMEM((count, rows, 128), F32)

    def array(*shape):
        return jax.ShapeDtypeStruct(shape, F32)

    operands = [
        pltpu.with_memory_space_constraint(x, pltpu.HBM)
        for x in (
            prior_cov,
            kern,
            offsets,
            obs_noise.reshape(1, 128),
            background.reshape(1, 128),
            observed.reshape(1, 128),
        )
    ]
    solved, vectors, prior_copy, pieces = pl.pallas_call(
        kernel,
        name="analysis",
        out_shape=(array(128, 128), array(2, 8, 128), array(512, 128), array(32, 16, 128)),
        in_specs=[hbm] * 6,
        out_specs=(vmem,) * 4,
        scratch_shapes=[
            pltpu.SMEM((128,), jnp.int32),
            tiles(3, 1),
            tiles(CHUNKS, GAP),
            tiles(CHUNKS, GAP),
            pltpu.VMEM((8 * STRIDE, 128), F32),
            tiles(16), tiles(32), tiles(2), tiles(8), tiles(16),
            tiles(2, 1), tiles(8, 1), tiles(4, 1),
            tiles(8, 16), tiles(8, 16), tiles(1, 16), tiles(8, 16),
            dma((6,)),
            dma((M // GROUP,)),
            pltpu.SemaphoreType.REGULAR,
        ]
        + [dma] * 18,
        compiler_params=pltpu.CompilerParams(
            collective_id=0, has_side_effects=True, vmem_limit_bytes=40 * 1024 * 1024
        ),
    )(*operands)
    ana, post = pl.pallas_call(
        finish,
        name="finish",
        out_shape=(array(1, 128), array(512, 128)),
        in_specs=[vmem] * 4,
        out_specs=(hbm, hbm),
        scratch_shapes=[
            pltpu.VMEM((1, 128), F32), pltpu.VMEM((512, 128), F32), dma((5,)),
        ],
        compiler_params=pltpu.CompilerParams(vmem_limit_bytes=40 * 1024 * 1024),
    )(solved, vectors, prior_copy, pieces)
    return ana.reshape(128), post


def solution(mesh):
    placed = (P("row", "col"), P(), P(), P(), P("col"), P())
    return jax.shard_map(
        on_device,
        mesh=mesh,
        in_specs=placed,
        out_specs=(P("col"), P("row", "col")),
        check_vma=False,
    )
```

```python
import jax
import jax.numpy as jnp
from jax import lax
from jax.experimental import pallas as pl
from jax.experimental.pallas import tpu as pltpu
from jax.sharding import PartitionSpec as P

MESH = pl.DeviceIdType.MESH
F32 = jnp.float32
M = 128
LOW = 24
CHUNKS = 64
STRIDE = 136
GROUP = 64
GAP = GROUP + 8


def ring(d, n):
    return min(d, n - d)


PLANE_STEPS = sorted(
    ((dx, dy) for dx in range(4) for dy in range(4) if dx or dy), key=lambda d: -ring(d[0], 4) - ring(d[1], 4)
)
PLANES_STEPS = sorted(range(1, 8), key=lambda d: -ring(d, 8))
PIVOTS = 16


def mm(a, b):
    return jnp.dot(a, b, precision=lax.Precision.HIGHEST, preferred_element_type=F32)


def mm_nt(a, b):
    return lax.dot_general(
        a, b, (((1,), (1,)), ((), ())), precision=lax.Precision.HIGHEST, preferred_element_type=F32
    )


def row_of(x, p):
    return jnp.broadcast_to(x[p : p + 1, :], x.shape)


def col_of(x, j):
    return jnp.broadcast_to(x[:, j : j + 1], x.shape)


def spd_inverse(blocks, b):
    count = M // b
    lane = lax.broadcasted_iota(jnp.int32, (b, M), 1)
    sub = lax.broadcasted_iota(jnp.int32, (b, M), 0)
    ahead = blocks[0]
    for k in range(count):
        inside = (lane >= k * b) & (lane < (k + 1) * b)
        cols = [col_of(ahead, k * b + j) for j in range(b)]
        top = jnp.where(inside, jnp.where(lane - k * b == sub, 1.0, 0.0), ahead)
        for p in range(b):
            scale = 1.0 / row_of(cols[p], p)
            is_p = sub == p
            t = row_of(top, p) * scale
            top = jnp.where(is_p, t, top - cols[p] * t)
            for j in range(p + 1, b):
                t = row_of(cols[j], p) * scale
                cols[j] = jnp.where(is_p, t, cols[j] - cols[p] * t)
        following = None
        if k + 1 < count:
            old = blocks[k + 1]
            following = jnp.where(inside, 0.0, old)
            for j in range(b):
                following = following - col_of(old, k * b + j) * row_of(top, j)
        parts = [top]
        if k:
            parts.insert(0, jnp.zeros((k * b, M), F32))
        if k + 1 < count:
            parts.append(jnp.zeros((M - (k + 1) * b, M), F32))
        update = mm(jnp.concatenate(blocks, 0), jnp.concatenate(parts, 0))
        new = []
        for i in range(count):
            if i == k:
                new.append(top)
            elif i == k + 1:
                new.append(following)
            else:
                new.append(jnp.where(inside, 0.0, blocks[i]) - update[i * b : (i + 1) * b])
        blocks, ahead = new, following
    return jnp.concatenate(blocks, 0)


def tree_sum(terms):
    while len(terms) > 1:
        terms = [sum(terms[i : i + 2][1:], terms[i]) for i in range(0, len(terms), 2)]
    return terms[0]


def kernel(
    prior_hbm, kernel_hbm, off_hbm, noise_hbm, bg_hbm, obs_hbm,
    solved_ref, vectors_ref, pv, g_row,
    off_ref, vec, kpad_0, kpad_1, hall,
    s_src, s_rs, z_src, z_rs, s_fin, m_src, m_rs, m_all, g_src, g_rs, g_sl, g_col,
    load_sem, group_sem, ready,
    s_send, s_recv, z_send, z_recv, f_send, f_recv, m_send, m_recv, ma_send, ma_recv,
    gs_send, gs_recv, gc_send, gc_recv, gr_send, gr_recv, sb_send, sb_recv,
):
    r = lax.axis_index("row")
    c = lax.axis_index("col")
    z = c // 4
    y_hi = (c // 2) % 2
    core = c % 2
    q = r * 2 + y_hi
    p = q * 2 + core
    owner = core == y_hi

    x = r // 2
    y = y_hi * 2 + r % 2

    def chip(dx, dy):
        to_x, to_y = (x + dx) % 4, (y + dy) % 4
        return to_x * 2 + to_y % 2, to_y // 2

    def plane(i):
        return (i // 4, z * 4 + i % 4)

    def send(source, target, send_sem, recv_sem, device):
        pltpu.make_async_remote_copy(
            source, target, send_sem, recv_sem, device_id=device, device_id_type=MESH
        ).start()

    def total(buffer, count, send_sem, recv_sem):
        view = buffer.at[pl.ds(0, count)]
        return pltpu.make_async_remote_copy(
            view, view, send_sem, recv_sem, device_id=(r, c), device_id_type=MESH
        )

    barrier = pltpu.get_barrier_semaphore()

    def greet(device):
        pl.semaphore_signal(barrier, inc=1, device_id=device, device_id_type=MESH)

    greetings = [(ring(dz, 8) + 0.5, (r, (c + 4 * dz) % 32)) for dz in range(1, 8)]
    for dx, dy in PLANE_STEPS:
        row, half = chip(dx, dy)
        for other in (0, 1):
            greetings.append((ring(dx, 4) + ring(dy, 4), (row, z * 4 + half * 2 + other)))
    greetings.sort(key=lambda g: -g[0])
    greetings = [device for _, device in greetings] + [(r, c + 1 - 2 * core)]
    for device in greetings[:16]:
        greet(device)

    off_copy = pltpu.make_async_copy(off_hbm, off_ref, load_sem.at[0])
    off_copy.start()
    kpads = (kpad_0, kpad_1)
    for group in range(M // GROUP):
        rows = pl.ds(group * GROUP, GROUP)
        for k in range(16):
            pltpu.make_async_copy(
                kernel_hbm.at[rows, pl.ds(k * 128, 128)], kpads[group].at[LOW + k, pl.ds(0, GROUP)], group_sem.at[group]
            ).start()
        if group == 0:
            for device in greetings[16:]:
                greet(device)
    prior_copy = pltpu.make_async_copy(prior_hbm, pv, load_sem.at[2])
    prior_copy.start()
    vec_copies = [
        pltpu.make_async_copy(source, vec.at[i], load_sem.at[3 + i])
        for i, source in enumerate((noise_hbm, bg_hbm, obs_hbm))
    ]
    for copy in vec_copies:
        copy.start()

    zeros = jnp.zeros((GROUP, 128), F32)
    for start, stop in ((LOW - 17, LOW), (LOW + 16, LOW + 32)):
        @pl.loop(start, stop)
        def _(i):
            for kpad in kpads:
                kpad[i, 0:GROUP] = zeros

    off_copy.wait()

    lane = lax.broadcasted_iota(jnp.int32, (8, 128), 1)
    sub = lax.broadcasted_iota(jnp.int32, (8, 128), 0)

    for group in range(M // GROUP):
        data = kpads[group].at[pl.ds(LOW, 16), pl.ds(0, GROUP)]
        flat = kpads[group].reshape(CHUNKS * GAP, 128)
        pltpu.make_async_copy(data, data, group_sem.at[group]).wait()
        built = []
        for u in range(GROUP):
            m = group * GROUP + u
            off = off_ref[m]
            chunk = lax.shift_right_logical(off, 7)
            turn = lax.bitwise_and(off, 127)
            at_r = (LOW + 4 * r - chunk) * GAP + u
            at_c = (LOW + c - chunk) * GAP + u
            now = jnp.where(
                sub < 4, flat[pl.ds(at_r, 8, stride=GAP), :], flat[pl.ds(at_c, 8, stride=0), :]
            )
            before = jnp.where(
                sub < 4,
                flat[pl.ds(at_r - GAP, 8, stride=GAP), :],
                flat[pl.ds(at_c - GAP, 8, stride=0), :],
            )
            turned = pltpu.roll(jnp.where(lane >= 128 - turn, before, now), turn, axis=1)
            built.append((m, turned))
        for m, turned in built:
            hall[pl.ds(m, 8, stride=STRIDE), :] = turned

    prior_copy.wait()
    h_r = jnp.concatenate([hall[j * STRIDE : j * STRIDE + 128, :] for j in range(4)], 1)
    part = mm(h_r, pv[...])
    h_c = hall[4 * STRIDE : 4 * STRIDE + 128, :]
    s_src[...] = mm_nt(h_c, part).reshape(16, 8, 128)

    pl.semaphore_wait(barrier, 38)

    for dx, dy in PLANE_STEPS:
        row, half = chip(dx, dy)
        to = row * 2 + half
        send(s_src.at[to], s_rs.at[p], s_send, s_recv, (row, z * 4 + half * 3))

    @pl.when(owner)
    def _():
        s_rs[p] = s_src[q]

    @pl.when(jnp.logical_not(owner))
    def _():
        send(s_src.at[q], s_rs.at[p], s_send, s_recv, (r, z * 4 + y_hi * 3))

    g_src[...] = jnp.transpose(part).reshape(8, 16, 128)
    g_rs[r] = g_src[r]

    @pl.loop(1, 8)
    def _(i):
        to = (r + i) % 8
        send(g_src.at[to], g_rs.at[r], gs_send, gs_recv, (to, c))

    for copy in vec_copies:
        copy.wait()
    mean = mm_nt(jnp.broadcast_to(vec[1], (8, 128)), h_c)[0:1, :]
    m_src[0] = mean
    m_rs[z] = mean

    @pl.loop(1, 8)
    def _(i):
        send(m_src.at[0], m_rs.at[z], m_send, m_recv, (r, (c + 4 * i) % 32))

    @pl.loop(0, 8)
    def _(i):
        pl.semaphore_signal(
            ready, inc=1, device_id=(i, z * 4 + (1 - y_hi) * 2 + core), device_id_type=MESH
        )

    @pl.when(owner)
    def _():
        total(s_rs, 31, s_send, s_recv).wait_recv()
        tile = tree_sum([s_rs[i] for i in range(32)])
        z_src[0] = tile
        z_rs[z] = tile
        for dz in PLANES_STEPS:
            send(z_src.at[0], z_rs.at[z], z_send, z_recv, (r, (c + 4 * dz) % 32))

    total(g_rs, 7, gs_send, gs_recv).wait_recv()
    pl.semaphore_wait(ready, 8)
    piece = tree_sum([g_rs[i] for i in range(8)])
    g_sl[0] = piece
    g_col[r] = piece
    slot = core * 16 + y_hi * 8 + r

    @pl.loop(1, 16)
    def _(i):
        to = (z * 2 + y_hi + i) % 16
        send(g_sl.at[0], g_row.at[slot], gr_send, gr_recv, (z, (to // 2) * 4 + (to % 2) * 2 + core))

    @pl.when(z == r)
    def _():
        pltpu.make_async_copy(g_sl.at[0], g_row.at[slot], gr_recv).start()

    @pl.when(z != r)
    def _():
        send(g_sl.at[0], g_row.at[slot], gr_send, gr_recv, (z, c))

    @pl.loop(1, 8)
    def _(i):
        send(g_sl.at[0], g_col.at[r], gc_send, gc_recv, ((r + i) % 8, c))

    @pl.when(owner)
    def _():
        total(z_rs, 7, z_send, z_recv).wait_recv()
        tile = tree_sum([z_rs[i] for i in range(8)])
        z_src[1] = tile
        s_fin[q] = tile

        for dx, dy in PLANE_STEPS + [(0, 0)]:
            row, half = chip(dx, dy)
            for other in (0, 1):
                if dx or dy:
                    to = (row, z * 4 + half * 2 + other)
                elif other:
                    to = (r, c + 1 - 2 * core)
                else:
                    continue
                send(z_src.at[1], s_fin.at[q], f_send, f_recv, to)

    total(m_rs, 7, m_send, m_recv).wait_recv()
    m_src[1] = tree_sum([m_rs[i] for i in range(8)])
    place = y_hi * 2 + core
    m_all[place] = m_src[1]

    @pl.loop(1, 4)
    def _(i):
        send(m_src.at[1], m_all.at[place], ma_send, ma_recv, (r, z * 4 + (place + i) % 4))

    total(g_row, 16, gr_send, gr_recv).wait_recv()
    half = g_row.at[pl.ds(core * 16, 16)]
    share = pltpu.make_async_remote_copy(
        half, half, sb_send, sb_recv, device_id=(r, c + 1 - 2 * core), device_id_type=MESH
    )
    share.start()

    @pl.when(owner)
    def _():
        total(s_fin, 15, f_send, f_recv).wait_recv()

    @pl.when(jnp.logical_not(owner))
    def _():
        total(s_fin, 16, f_send, f_recv).wait_recv()

    rows = lax.broadcasted_iota(jnp.int32, (128, 128), 0)
    lanes = lax.broadcasted_iota(jnp.int32, (128, 128), 1)
    noise = jnp.where(rows == lanes, jnp.broadcast_to(vec[0], (128, 128)), 0.0)
    s_all = s_fin[...].reshape(128, 128) + noise
    total(g_col, 7, gc_send, gc_recv).wait_recv()
    g_c = jnp.transpose(g_col[...].reshape(128, 128))
    inverse = spd_inverse([s_all[i * PIVOTS : (i + 1) * PIVOTS] for i in range(M // PIVOTS)], PIVOTS)

    total(m_all, 3, ma_send, ma_recv).wait_recv()
    mean = tree_sum([m_all[i] for i in range(4)])
    vectors_ref[0] = jnp.broadcast_to(vec[2] - mean, (8, 128))
    vectors_ref[1] = jnp.broadcast_to(vec[1], (8, 128))

    solved_ref[...] = mm(inverse, g_c)

    share.wait_recv()

    @pl.when(owner)
    def _():
        total(s_rs, 15, s_send, s_recv).wait_send()
        total(z_rs, 7, z_send, z_recv).wait_send()
        total(s_rs, 31, f_send, f_recv).wait_send()

    @pl.when(jnp.logical_not(owner))
    def _():
        total(s_rs, 16, s_send, s_recv).wait_send()

    total(m_rs, 7, m_send, m_recv).wait_send()
    total(m_all, 3, ma_send, ma_recv).wait_send()
    total(g_rs, 7, gs_send, gs_recv).wait_send()
    total(g_col, 7, gc_send, gc_recv).wait_send()
    share.wait_send()

    @pl.when(z == r)
    def _():
        total(g_row, 15, gr_send, gr_recv).wait_send()

    @pl.when(z != r)
    def _():
        total(g_row, 16, gr_send, gr_recv).wait_send()


def finish(solved_ref, vectors_ref, pv, g_row, ana_hbm, post_hbm, ana, post, sem):
    solved = solved_ref[...]
    ana[...] = (vectors_ref[1] + mm(vectors_ref[0], solved))[0:1, :]
    copies = [pltpu.make_async_copy(ana, ana_hbm, sem.at[4])]
    copies[0].start()
    for j in range(4):
        first = (j % 2) * 16 + (j // 2) * 8
        g_j = g_row[first : first + 8].reshape(128, 128)
        here = slice(j * 128, (j + 1) * 128)
        post[here, :] = pv[here, :] - mm(g_j, solved)
        copies.append(pltpu.make_async_copy(post.at[here], post_hbm.at[here], sem.at[j]))
        copies[-1].start()
    for copy in copies:
        copy.wait()


def on_device(prior_cov, kern, offsets, obs_noise, background, observed):
    vmem = pl.BlockSpec(memory_space=pltpu.VMEM)
    hbm = pl.BlockSpec(memory_space=pltpu.HBM)
    dma = pltpu.SemaphoreType.DMA

    def tiles(count, rows=8):
        return pltpu.VMEM((count, rows, 128), F32)

    def array(*shape):
        return jax.ShapeDtypeStruct(shape, F32)

    operands = [
        pltpu.with_memory_space_constraint(x, pltpu.HBM)
        for x in (
            prior_cov,
            kern,
            offsets,
            obs_noise.reshape(1, 128),
            background.reshape(1, 128),
            observed.reshape(1, 128),
        )
    ]
    solved, vectors, prior_copy, pieces = pl.pallas_call(
        kernel,
        name="analysis",
        out_shape=(array(128, 128), array(2, 8, 128), array(512, 128), array(32, 16, 128)),
        in_specs=[hbm] * 6,
        out_specs=(vmem,) * 4,
        scratch_shapes=[
            pltpu.SMEM((128,), jnp.int32),
            tiles(3, 1),
            tiles(CHUNKS, GAP),
            tiles(CHUNKS, GAP),
            pltpu.VMEM((8 * STRIDE, 128), F32),
            tiles(16), tiles(32), tiles(2), tiles(8), tiles(16),
            tiles(2, 1), tiles(8, 1), tiles(4, 1),
            tiles(8, 16), tiles(8, 16), tiles(1, 16), tiles(8, 16),
            dma((6,)),
            dma((M // GROUP,)),
            pltpu.SemaphoreType.REGULAR,
        ]
        + [dma] * 18,
        compiler_params=pltpu.CompilerParams(
            collective_id=0, has_side_effects=True, vmem_limit_bytes=40 * 1024 * 1024
        ),
    )(*operands)
    ana, post = pl.pallas_call(
        finish,
        name="finish",
        out_shape=(array(1, 128), array(512, 128)),
        in_specs=[vmem] * 4,
        out_specs=(hbm, hbm),
        scratch_shapes=[
            pltpu.VMEM((1, 128), F32), pltpu.VMEM((512, 128), F32), dma((5,)),
        ],
        compiler_params=pltpu.CompilerParams(vmem_limit_bytes=40 * 1024 * 1024),
    )(solved, vectors, prior_copy, pieces)
    return ana.reshape(128), post


def solution(mesh):
    placed = (P("row", "col"), P(), P(), P(), P("col"), P())
    return jax.shard_map(
        on_device,
        mesh=mesh,
        in_specs=placed,
        out_specs=(P("col"), P("row", "col")),
        check_vma=False,
    )
```

```python
import jax
import jax.numpy as jnp
from jax import lax
from jax.experimental import pallas as pl
from jax.experimental.pallas import tpu as pltpu
from jax.sharding import PartitionSpec as P

MESH = pl.DeviceIdType.MESH
F32 = jnp.float32
M = 128
LOW = 24
CHUNKS = 64
STRIDE = 136
GROUP = 64
GAP = GROUP + 8


def ring(d, n):
    return min(d, n - d)


PLANE_STEPS = sorted(
    ((dx, dy) for dx in range(4) for dy in range(4) if dx or dy), key=lambda d: -ring(d[0], 4) - ring(d[1], 4)
)
PLANES_STEPS = sorted(range(1, 8), key=lambda d: -ring(d, 8))
PIVOTS = 16


def mm(a, b):
    return jnp.dot(a, b, precision=lax.Precision.HIGHEST, preferred_element_type=F32)


def mm_nt(a, b):
    return lax.dot_general(
        a, b, (((1,), (1,)), ((), ())), precision=lax.Precision.HIGHEST, preferred_element_type=F32
    )


def row_of(x, p):
    return jnp.broadcast_to(x[p : p + 1, :], x.shape)


def col_of(x, j):
    return jnp.broadcast_to(x[:, j : j + 1], x.shape)


def spd_inverse(blocks, b):
    count = M // b
    lane = lax.broadcasted_iota(jnp.int32, (b, M), 1)
    sub = lax.broadcasted_iota(jnp.int32, (b, M), 0)
    ahead = blocks[0]
    for k in range(count):
        inside = (lane >= k * b) & (lane < (k + 1) * b)
        cols = [col_of(ahead, k * b + j) for j in range(b)]
        top = jnp.where(inside, jnp.where(lane - k * b == sub, 1.0, 0.0), ahead)
        for p in range(b):
            scale = 1.0 / row_of(cols[p], p)
            is_p = sub == p
            t = row_of(top, p) * scale
            top = jnp.where(is_p, t, top - cols[p] * t)
            for j in range(p + 1, b):
                t = row_of(cols[j], p) * scale
                cols[j] = jnp.where(is_p, t, cols[j] - cols[p] * t)
        following = None
        if k + 1 < count:
            old = blocks[k + 1]
            following = jnp.where(inside, 0.0, old)
            for j in range(b):
                following = following - col_of(old, k * b + j) * row_of(top, j)
        parts = [top]
        if k:
            parts.insert(0, jnp.zeros((k * b, M), F32))
        if k + 1 < count:
            parts.append(jnp.zeros((M - (k + 1) * b, M), F32))
        update = mm(jnp.concatenate(blocks, 0), jnp.concatenate(parts, 0))
        new = []
        for i in range(count):
            if i == k:
                new.append(top)
            elif i == k + 1:
                new.append(following)
            else:
                new.append(jnp.where(inside, 0.0, blocks[i]) - update[i * b : (i + 1) * b])
        blocks, ahead = new, following
    return jnp.concatenate(blocks, 0)


def tree_sum(terms):
    while len(terms) > 1:
        terms = [sum(terms[i : i + 2][1:], terms[i]) for i in range(0, len(terms), 2)]
    return terms[0]


def kernel(
    prior_hbm, kernel_hbm, off_hbm, noise_hbm, bg_hbm, obs_hbm,
    solved_ref, vectors_ref, pv, g_row,
    off_ref, vec, kpad_0, kpad_1, hall,
    s_src, s_rs, z_src, z_rs, s_fin, m_src, m_rs, m_all, g_src, g_rs, g_sl, g_col,
    load_sem, group_sem, ready,
    s_send, s_recv, z_send, z_recv, f_send, f_recv, m_send, m_recv, ma_send, ma_recv,
    gs_send, gs_recv, gc_send, gc_recv, gr_send, gr_recv, sb_send, sb_recv,
):
    r = lax.axis_index("row")
    c = lax.axis_index("col")
    z = c // 4
    y_hi = (c // 2) % 2
    core = c % 2
    q = r * 2 + y_hi
    p = q * 2 + core
    owner = core == y_hi

    x = r // 2
    y = y_hi * 2 + r % 2

    def chip(dx, dy):
        to_x, to_y = (x + dx) % 4, (y + dy) % 4
        return to_x * 2 + to_y % 2, to_y // 2

    def plane(i):
        return (i // 4, z * 4 + i % 4)

    def send(source, target, send_sem, recv_sem, device):
        pltpu.make_async_remote_copy(
            source, target, send_sem, recv_sem, device_id=device, device_id_type=MESH
        ).start()

    def total(buffer, count, send_sem, recv_sem):
        view = buffer.at[pl.ds(0, count)]
        return pltpu.make_async_remote_copy(
            view, view, send_sem, recv_sem, device_id=(r, c), device_id_type=MESH
        )

    barrier = pltpu.get_barrier_semaphore()

    def greet(device):
        pl.semaphore_signal(barrier, inc=1, device_id=device, device_id_type=MESH)

    greetings = [(ring(dz, 8) + 0.5, (r, (c + 4 * dz) % 32)) for dz in range(1, 8)]
    for dx, dy in PLANE_STEPS:
        row, half = chip(dx, dy)
        for other in (0, 1):
            greetings.append((ring(dx, 4) + ring(dy, 4), (row, z * 4 + half * 2 + other)))
    greetings.sort(key=lambda g: -g[0])
    greetings = [device for _, device in greetings] + [(r, c + 1 - 2 * core)]
    for device in greetings[:16]:
        greet(device)

    off_copy = pltpu.make_async_copy(off_hbm, off_ref, load_sem.at[0])
    off_copy.start()
    kpads = (kpad_0, kpad_1)
    for group in range(M // GROUP):
        rows = pl.ds(group * GROUP, GROUP)
        for k in range(16):
            pltpu.make_async_copy(
                kernel_hbm.at[rows, pl.ds(k * 128, 128)], kpads[group].at[LOW + k, pl.ds(0, GROUP)], group_sem.at[group]
            ).start()
        if group == 0:
            for device in greetings[16:]:
                greet(device)
    prior_copy = pltpu.make_async_copy(prior_hbm, pv, load_sem.at[2])
    prior_copy.start()
    vec_copies = [
        pltpu.make_async_copy(source, vec.at[i], load_sem.at[3 + i])
        for i, source in enumerate((noise_hbm, bg_hbm, obs_hbm))
    ]
    for copy in vec_copies:
        copy.start()

    zeros = jnp.zeros((GROUP, 128), F32)
    for start, stop in ((LOW - 17, LOW), (LOW + 16, LOW + 32)):
        @pl.loop(start, stop)
        def _(i):
            for kpad in kpads:
                kpad[i, 0:GROUP] = zeros

    off_copy.wait()

    lane = lax.broadcasted_iota(jnp.int32, (8, 128), 1)
    sub = lax.broadcasted_iota(jnp.int32, (8, 128), 0)

    for group in range(M // GROUP):
        data = kpads[group].at[pl.ds(LOW, 16), pl.ds(0, GROUP)]
        flat = kpads[group].reshape(CHUNKS * GAP, 128)
        pltpu.make_async_copy(data, data, group_sem.at[group]).wait()
        built = []
        for u in range(GROUP):
            m = group * GROUP + u
            off = off_ref[m]
            chunk = lax.shift_right_logical(off, 7)
            turn = lax.bitwise_and(off, 127)
            at_r = (LOW + 4 * r - chunk) * GAP + u
            at_c = (LOW + c - chunk) * GAP + u
            now = jnp.where(
                sub < 4, flat[pl.ds(at_r, 8, stride=GAP), :], flat[pl.ds(at_c, 8, stride=0), :]
            )
            before = jnp.where(
                sub < 4,
                flat[pl.ds(at_r - GAP, 8, stride=GAP), :],
                flat[pl.ds(at_c - GAP, 8, stride=0), :],
            )
            turned = pltpu.roll(jnp.where(lane >= 128 - turn, before, now), turn, axis=1)
            built.append((m, turned))
        for m, turned in built:
            hall[pl.ds(m, 8, stride=STRIDE), :] = turned

    prior_copy.wait()
    h_r = jnp.concatenate([hall[j * STRIDE : j * STRIDE + 128, :] for j in range(4)], 1)
    part = mm(h_r, pv[...])
    h_c = hall[4 * STRIDE : 4 * STRIDE + 128, :]
    s_src[...] = mm_nt(h_c, part).reshape(16, 8, 128)

    pl.semaphore_wait(barrier, 38)

    for dx, dy in PLANE_STEPS:
        row, half = chip(dx, dy)
        to = row * 2 + half
        send(s_src.at[to], s_rs.at[p], s_send, s_recv, (row, z * 4 + half * 3))

    @pl.when(owner)
    def _():
        s_rs[p] = s_src[q]

    @pl.when(jnp.logical_not(owner))
    def _():
        send(s_src.at[q], s_rs.at[p], s_send, s_recv, (r, z * 4 + y_hi * 3))

    g_src[...] = jnp.transpose(part).reshape(8, 16, 128)
    g_rs[r] = g_src[r]

    @pl.loop(1, 8)
    def _(i):
        to = (r + i) % 8
        send(g_src.at[to], g_rs.at[r], gs_send, gs_recv, (to, c))

    for copy in vec_copies:
        copy.wait()
    mean = mm_nt(jnp.broadcast_to(vec[1], (8, 128)), h_c)[0:1, :]
    m_src[0] = mean
    m_rs[z] = mean

    @pl.loop(1, 8)
    def _(i):
        send(m_src.at[0], m_rs.at[z], m_send, m_recv, (r, (c + 4 * i) % 32))

    @pl.loop(0, 8)
    def _(i):
        pl.semaphore_signal(
            ready, inc=1, device_id=(i, z * 4 + (1 - y_hi) * 2 + core), device_id_type=MESH
        )

    @pl.when(owner)
    def _():
        total(s_rs, 31, s_send, s_recv).wait_recv()
        tile = tree_sum([s_rs[i] for i in range(32)])
        z_src[0] = tile
        z_rs[z] = tile
        for dz in PLANES_STEPS:
            send(z_src.at[0], z_rs.at[z], z_send, z_recv, (r, (c + 4 * dz) % 32))

    total(g_rs, 7, gs_send, gs_recv).wait_recv()
    pl.semaphore_wait(ready, 8)
    piece = tree_sum([g_rs[i] for i in range(8)])
    g_sl[0] = piece
    g_col[r] = piece
    slot = core * 16 + y_hi * 8 + r

    for dz in PLANES_STEPS + [0]:
        for half in (0, 1) if dz else (1,):
            col = (z + dz) % 8 * 4 + (y_hi + half) % 2 * 2 + core
            send(g_sl.at[0], g_row.at[slot], gr_send, gr_recv, (z, col))

    @pl.when(z == r)
    def _():
        pltpu.make_async_copy(g_sl.at[0], g_row.at[slot], gr_recv).start()

    @pl.when(z != r)
    def _():
        send(g_sl.at[0], g_row.at[slot], gr_send, gr_recv, (z, c))

    @pl.loop(1, 8)
    def _(i):
        send(g_sl.at[0], g_col.at[r], gc_send, gc_recv, ((r + i) % 8, c))

    @pl.when(owner)
    def _():
        total(z_rs, 7, z_send, z_recv).wait_recv()
        tile = tree_sum([z_rs[i] for i in range(8)])
        z_src[1] = tile
        s_fin[q] = tile

        for dx, dy in PLANE_STEPS + [(0, 0)]:
            row, half = chip(dx, dy)
            for other in (0, 1):
                if dx or dy:
                    to = (row, z * 4 + half * 2 + other)
                elif other:
                    to = (r, c + 1 - 2 * core)
                else:
                    continue
                send(z_src.at[1], s_fin.at[q], f_send, f_recv, to)

    total(m_rs, 7, m_send, m_recv).wait_recv()
    m_src[1] = tree_sum([m_rs[i] for i in range(8)])
    place = y_hi * 2 + core
    m_all[place] = m_src[1]

    @pl.loop(1, 4)
    def _(i):
        send(m_src.at[1], m_all.at[place], ma_send, ma_recv, (r, z * 4 + (place + i) % 4))

    total(g_row, 16, gr_send, gr_recv).wait_recv()
    half = g_row.at[pl.ds(core * 16, 16)]
    share = pltpu.make_async_remote_copy(
        half, half, sb_send, sb_recv, device_id=(r, c + 1 - 2 * core), device_id_type=MESH
    )
    share.start()

    @pl.when(owner)
    def _():
        total(s_fin, 15, f_send, f_recv).wait_recv()

    @pl.when(jnp.logical_not(owner))
    def _():
        total(s_fin, 16, f_send, f_recv).wait_recv()

    rows = lax.broadcasted_iota(jnp.int32, (128, 128), 0)
    lanes = lax.broadcasted_iota(jnp.int32, (128, 128), 1)
    noise = jnp.where(rows == lanes, jnp.broadcast_to(vec[0], (128, 128)), 0.0)
    s_all = s_fin[...].reshape(128, 128) + noise
    total(g_col, 7, gc_send, gc_recv).wait_recv()
    g_c = jnp.transpose(g_col[...].reshape(128, 128))
    inverse = spd_inverse([s_all[i * PIVOTS : (i + 1) * PIVOTS] for i in range(M // PIVOTS)], PIVOTS)

    total(m_all, 3, ma_send, ma_recv).wait_recv()
    mean = tree_sum([m_all[i] for i in range(4)])
    vectors_ref[0] = jnp.broadcast_to(vec[2] - mean, (8, 128))
    vectors_ref[1] = jnp.broadcast_to(vec[1], (8, 128))

    solved_ref[...] = mm(inverse, g_c)

    share.wait_recv()

    @pl.when(owner)
    def _():
        total(s_rs, 15, s_send, s_recv).wait_send()
        total(z_rs, 7, z_send, z_recv).wait_send()
        total(s_rs, 31, f_send, f_recv).wait_send()

    @pl.when(jnp.logical_not(owner))
    def _():
        total(s_rs, 16, s_send, s_recv).wait_send()

    total(m_rs, 7, m_send, m_recv).wait_send()
    total(m_all, 3, ma_send, ma_recv).wait_send()
    total(g_rs, 7, gs_send, gs_recv).wait_send()
    total(g_col, 7, gc_send, gc_recv).wait_send()
    share.wait_send()

    @pl.when(z == r)
    def _():
        total(g_row, 15, gr_send, gr_recv).wait_send()

    @pl.when(z != r)
    def _():
        total(g_row, 16, gr_send, gr_recv).wait_send()


def finish(solved_ref, vectors_ref, pv, g_row, ana_hbm, post_hbm, ana, post, sem):
    solved = solved_ref[...]
    copies = []
    for j in range(4):
        first = (j % 2) * 16 + (j // 2) * 8
        g_j = g_row[first : first + 8].reshape(128, 128)
        here = slice(j * 128, (j + 1) * 128)
        if j == 0:
            both = mm(jnp.concatenate([vectors_ref[0], g_j], 0), solved)
            change = both[8:, :]
            ana[...] = (vectors_ref[1] + both[:8, :])[0:1, :]
            copies.append(pltpu.make_async_copy(ana, ana_hbm, sem.at[4]))
            copies[-1].start()
        else:
            change = mm(g_j, solved)
        post[here, :] = pv[here, :] - change
        copies.append(pltpu.make_async_copy(post.at[here], post_hbm.at[here], sem.at[j]))
        copies[-1].start()
    for copy in copies:
        copy.wait()


def on_device(prior_cov, kern, offsets, obs_noise, background, observed):
    vmem = pl.BlockSpec(memory_space=pltpu.VMEM)
    hbm = pl.BlockSpec(memory_space=pltpu.HBM)
    dma = pltpu.SemaphoreType.DMA

    def tiles(count, rows=8):
        return pltpu.VMEM((count, rows, 128), F32)

    def array(*shape):
        return jax.ShapeDtypeStruct(shape, F32)

    operands = [
        pltpu.with_memory_space_constraint(x, pltpu.HBM)
        for x in (
            prior_cov,
            kern,
            offsets,
            obs_noise.reshape(1, 128),
            background.reshape(1, 128),
            observed.reshape(1, 128),
        )
    ]
    solved, vectors, prior_copy, pieces = pl.pallas_call(
        kernel,
        name="analysis",
        out_shape=(array(128, 128), array(2, 8, 128), array(512, 128), array(32, 16, 128)),
        in_specs=[hbm] * 6,
        out_specs=(vmem,) * 4,
        scratch_shapes=[
            pltpu.SMEM((128,), jnp.int32),
            tiles(3, 1),
            tiles(CHUNKS, GAP),
            tiles(CHUNKS, GAP),
            pltpu.VMEM((8 * STRIDE, 128), F32),
            tiles(16), tiles(32), tiles(2), tiles(8), tiles(16),
            tiles(2, 1), tiles(8, 1), tiles(4, 1),
            tiles(8, 16), tiles(8, 16), tiles(1, 16), tiles(8, 16),
            dma((6,)),
            dma((M // GROUP,)),
            pltpu.SemaphoreType.REGULAR,
        ]
        + [dma] * 18,
        compiler_params=pltpu.CompilerParams(
            collective_id=0, has_side_effects=True, vmem_limit_bytes=40 * 1024 * 1024
        ),
    )(*operands)
    ana, post = pl.pallas_call(
        finish,
        name="finish",
        out_shape=(array(1, 128), array(512, 128)),
        in_specs=[vmem] * 4,
        out_specs=(hbm, hbm),
        scratch_shapes=[
            pltpu.VMEM((1, 128), F32), pltpu.VMEM((512, 128), F32), dma((5,)),
        ],
        compiler_params=pltpu.CompilerParams(vmem_limit_bytes=40 * 1024 * 1024),
    )(solved, vectors, prior_copy, pieces)
    return ana.reshape(128), post


def solution(mesh):
    placed = (P("row", "col"), P(), P(), P(), P("col"), P())
    return jax.shard_map(
        on_device,
        mesh=mesh,
        in_specs=placed,
        out_specs=(P("col"), P("row", "col")),
        check_vma=False,
    )
```

```python
import jax
import jax.numpy as jnp
from jax import lax
from jax.experimental import pallas as pl
from jax.experimental.pallas import tpu as pltpu
from jax.sharding import PartitionSpec as P

MESH = pl.DeviceIdType.MESH
F32 = jnp.float32
M = 128
LOW = 24
CHUNKS = 64
STRIDE = 136
GROUP = 64
GAP = GROUP + 8


def ring(d, n):
    return min(d, n - d)


PLANE_STEPS = sorted(
    ((dx, dy) for dx in range(4) for dy in range(4) if dx or dy), key=lambda d: -ring(d[0], 4) - ring(d[1], 4)
)
PLANES_STEPS = sorted(range(1, 8), key=lambda d: -ring(d, 8))
PIVOTS = 16


def mm(a, b):
    return jnp.dot(a, b, precision=lax.Precision.HIGHEST, preferred_element_type=F32)


def mm_nt(a, b):
    return lax.dot_general(
        a, b, (((1,), (1,)), ((), ())), precision=lax.Precision.HIGHEST, preferred_element_type=F32
    )


def row_of(x, p):
    return jnp.broadcast_to(x[p : p + 1, :], x.shape)


def col_of(x, j):
    return jnp.broadcast_to(x[:, j : j + 1], x.shape)


def spd_inverse(blocks, b):
    count = M // b
    lane = lax.broadcasted_iota(jnp.int32, (b, M), 1)
    sub = lax.broadcasted_iota(jnp.int32, (b, M), 0)
    ahead = blocks[0]
    for k in range(count):
        inside = (lane >= k * b) & (lane < (k + 1) * b)
        cols = [col_of(ahead, k * b + j) for j in range(b)]
        top = jnp.where(inside, jnp.where(lane - k * b == sub, 1.0, 0.0), ahead)
        for p in range(b):
            scale = 1.0 / row_of(cols[p], p)
            is_p = sub == p
            t = row_of(top, p) * scale
            top = jnp.where(is_p, t, top - cols[p] * t)
            for j in range(p + 1, b):
                t = row_of(cols[j], p) * scale
                cols[j] = jnp.where(is_p, t, cols[j] - cols[p] * t)
        following = None
        if k + 1 < count:
            old = blocks[k + 1]
            following = jnp.where(inside, 0.0, old)
            for j in range(b):
                following = following - col_of(old, k * b + j) * row_of(top, j)
        parts = [top]
        if k:
            parts.insert(0, jnp.zeros((k * b, M), F32))
        if k + 1 < count:
            parts.append(jnp.zeros((M - (k + 1) * b, M), F32))
        update = mm(jnp.concatenate(blocks, 0), jnp.concatenate(parts, 0))
        new = []
        for i in range(count):
            if i == k:
                new.append(top)
            elif i == k + 1:
                new.append(following)
            else:
                new.append(jnp.where(inside, 0.0, blocks[i]) - update[i * b : (i + 1) * b])
        blocks, ahead = new, following
    return jnp.concatenate(blocks, 0)


def tree_sum(terms):
    while len(terms) > 1:
        terms = [sum(terms[i : i + 2][1:], terms[i]) for i in range(0, len(terms), 2)]
    return terms[0]


def kernel(
    prior_hbm, kernel_hbm, off_hbm, noise_hbm, bg_hbm, obs_hbm,
    solved_ref, vectors_ref, pv, g_row,
    off_ref, vec, kpad_0, kpad_1, hall,
    s_src, s_rs, z_src, z_rs, s_fin, m_src, m_rs, m_all, g_src, g_rs, g_sl, g_col,
    load_sem, group_sem, ready,
    s_send, s_recv, z_send, z_recv, f_send, f_recv, m_send, m_recv, ma_send, ma_recv,
    gs_send, gs_recv, gc_send, gc_recv, gr_send, gr_recv, sb_send, sb_recv,
):
    r = lax.axis_index("row")
    c = lax.axis_index("col")
    z = c // 4
    y_hi = (c // 2) % 2
    core = c % 2
    q = r * 2 + y_hi
    p = q * 2 + core
    owner = core == y_hi

    x = r // 2
    y = y_hi * 2 + r % 2

    def chip(dx, dy):
        to_x, to_y = (x + dx) % 4, (y + dy) % 4
        return to_x * 2 + to_y % 2, to_y // 2

    def plane(i):
        return (i // 4, z * 4 + i % 4)

    def send(source, target, send_sem, recv_sem, device):
        pltpu.make_async_remote_copy(
            source, target, send_sem, recv_sem, device_id=device, device_id_type=MESH
        ).start()

    def total(buffer, count, send_sem, recv_sem):
        view = buffer.at[pl.ds(0, count)]
        return pltpu.make_async_remote_copy(
            view, view, send_sem, recv_sem, device_id=(r, c), device_id_type=MESH
        )

    barrier = pltpu.get_barrier_semaphore()

    def greet(device):
        pl.semaphore_signal(barrier, inc=1, device_id=device, device_id_type=MESH)

    greetings = [(ring(dz, 8) + 0.5, (r, (c + 4 * dz) % 32)) for dz in range(1, 8)]
    for dx, dy in PLANE_STEPS:
        row, half = chip(dx, dy)
        for other in (0, 1):
            greetings.append((ring(dx, 4) + ring(dy, 4), (row, z * 4 + half * 2 + other)))
    greetings.sort(key=lambda g: -g[0])
    greetings = [device for _, device in greetings] + [(r, c + 1 - 2 * core)]
    for device in greetings[:16]:
        greet(device)

    off_copy = pltpu.make_async_copy(off_hbm, off_ref, load_sem.at[0])
    off_copy.start()
    kpads = (kpad_0, kpad_1)
    for group in range(M // GROUP):
        rows = pl.ds(group * GROUP, GROUP)
        for k in range(16):
            pltpu.make_async_copy(
                kernel_hbm.at[rows, pl.ds(k * 128, 128)], kpads[group].at[LOW + k, pl.ds(0, GROUP)], group_sem.at[group]
            ).start()
        if group == 0:
            for device in greetings[16:]:
                greet(device)
    prior_copy = pltpu.make_async_copy(prior_hbm, pv, load_sem.at[2])
    prior_copy.start()
    vec_copies = [
        pltpu.make_async_copy(source, vec.at[i], load_sem.at[3 + i])
        for i, source in enumerate((noise_hbm, bg_hbm, obs_hbm))
    ]
    for copy in vec_copies:
        copy.start()

    zeros = jnp.zeros((GROUP, 128), F32)
    for start, stop in ((LOW - 17, LOW), (LOW + 16, LOW + 32)):
        @pl.loop(start, stop)
        def _(i):
            for kpad in kpads:
                kpad[i, 0:GROUP] = zeros

    off_copy.wait()

    lane = lax.broadcasted_iota(jnp.int32, (8, 128), 1)
    sub = lax.broadcasted_iota(jnp.int32, (8, 128), 0)

    for group in range(M // GROUP):
        data = kpads[group].at[pl.ds(LOW, 16), pl.ds(0, GROUP)]
        flat = kpads[group].reshape(CHUNKS * GAP, 128)
        pltpu.make_async_copy(data, data, group_sem.at[group]).wait()
        built = []
        for u in range(GROUP):
            m = group * GROUP + u
            off = off_ref[m]
            chunk = lax.shift_right_logical(off, 7)
            turn = lax.bitwise_and(off, 127)
            at_r = (LOW + 4 * r - chunk) * GAP + u
            at_c = (LOW + c - chunk) * GAP + u
            now = jnp.where(
                sub < 4, flat[pl.ds(at_r, 8, stride=GAP), :], flat[pl.ds(at_c, 8, stride=0), :]
            )
            before = jnp.where(
                sub < 4,
                flat[pl.ds(at_r - GAP, 8, stride=GAP), :],
                flat[pl.ds(at_c - GAP, 8, stride=0), :],
            )
            turned = pltpu.roll(jnp.where(lane >= 128 - turn, before, now), turn, axis=1)
            built.append((m, turned))
        for m, turned in built:
            hall[pl.ds(m, 8, stride=STRIDE), :] = turned

    prior_copy.wait()
    h_r = jnp.concatenate([hall[j * STRIDE : j * STRIDE + 128, :] for j in range(4)], 1)
    part = mm(h_r, pv[...])
    h_c = hall[4 * STRIDE : 4 * STRIDE + 128, :]
    s_src[...] = mm_nt(h_c, part).reshape(16, 8, 128)

    pl.semaphore_wait(barrier, 38)

    for dx, dy in PLANE_STEPS:
        row, half = chip(dx, dy)
        to = row * 2 + half
        send(s_src.at[to], s_rs.at[p], s_send, s_recv, (row, z * 4 + half * 3))

    @pl.when(owner)
    def _():
        s_rs[p] = s_src[q]

    @pl.when(jnp.logical_not(owner))
    def _():
        send(s_src.at[q], s_rs.at[p], s_send, s_recv, (r, z * 4 + y_hi * 3))

    g_src[...] = jnp.transpose(part).reshape(8, 16, 128)
    g_rs[r] = g_src[r]

    for dx, flip in ((2, 1), (1, 1), (3, 1), (2, 0), (1, 0), (3, 0), (0, 1)):
        to = (x + dx) % 4 * 2 + (r + flip) % 2
        send(g_src.at[to], g_rs.at[r], gs_send, gs_recv, (to, c))

    for copy in vec_copies:
        copy.wait()
    mean = mm_nt(jnp.broadcast_to(vec[1], (8, 128)), h_c)[0:1, :]
    m_src[0] = mean
    m_rs[z] = mean

    @pl.loop(1, 8)
    def _(i):
        send(m_src.at[0], m_rs.at[z], m_send, m_recv, (r, (c + 4 * i) % 32))

    @pl.loop(0, 8)
    def _(i):
        pl.semaphore_signal(
            ready, inc=1, device_id=(i, z * 4 + (1 - y_hi) * 2 + core), device_id_type=MESH
        )

    @pl.when(owner)
    def _():
        total(s_rs, 31, s_send, s_recv).wait_recv()
        tile = tree_sum([s_rs[i] for i in range(32)])
        z_src[0] = tile
        z_rs[z] = tile
        for dz in PLANES_STEPS:
            send(z_src.at[0], z_rs.at[z], z_send, z_recv, (r, (c + 4 * dz) % 32))

    total(g_rs, 7, gs_send, gs_recv).wait_recv()
    pl.semaphore_wait(ready, 8)
    piece = tree_sum([g_rs[i] for i in range(8)])
    g_sl[0] = piece
    g_col[r] = piece
    slot = core * 16 + y_hi * 8 + r

    for dz in PLANES_STEPS + [0]:
        for half in (0, 1) if dz else (1,):
            col = (z + dz) % 8 * 4 + (y_hi + half) % 2 * 2 + core
            send(g_sl.at[0], g_row.at[slot], gr_send, gr_recv, (z, col))

    @pl.when(z == r)
    def _():
        pltpu.make_async_copy(g_sl.at[0], g_row.at[slot], gr_recv).start()

    @pl.when(z != r)
    def _():
        send(g_sl.at[0], g_row.at[slot], gr_send, gr_recv, (z, c))

    @pl.loop(1, 8)
    def _(i):
        send(g_sl.at[0], g_col.at[r], gc_send, gc_recv, ((r + i) % 8, c))

    @pl.when(owner)
    def _():
        total(z_rs, 7, z_send, z_recv).wait_recv()
        tile = tree_sum([z_rs[i] for i in range(8)])
        z_src[1] = tile
        s_fin[q] = tile

        for dx, dy in PLANE_STEPS + [(0, 0)]:
            row, half = chip(dx, dy)
            for other in (0, 1):
                if dx or dy:
                    to = (row, z * 4 + half * 2 + other)
                elif other:
                    to = (r, c + 1 - 2 * core)
                else:
                    continue
                send(z_src.at[1], s_fin.at[q], f_send, f_recv, to)

    total(m_rs, 7, m_send, m_recv).wait_recv()
    m_src[1] = tree_sum([m_rs[i] for i in range(8)])
    place = y_hi * 2 + core
    m_all[place] = m_src[1]

    @pl.loop(1, 4)
    def _(i):
        send(m_src.at[1], m_all.at[place], ma_send, ma_recv, (r, z * 4 + (place + i) % 4))

    total(g_row, 16, gr_send, gr_recv).wait_recv()
    half = g_row.at[pl.ds(core * 16, 16)]
    share = pltpu.make_async_remote_copy(
        half, half, sb_send, sb_recv, device_id=(r, c + 1 - 2 * core), device_id_type=MESH
    )
    share.start()

    @pl.when(owner)
    def _():
        total(s_fin, 15, f_send, f_recv).wait_recv()

    @pl.when(jnp.logical_not(owner))
    def _():
        total(s_fin, 16, f_send, f_recv).wait_recv()

    rows = lax.broadcasted_iota(jnp.int32, (128, 128), 0)
    lanes = lax.broadcasted_iota(jnp.int32, (128, 128), 1)
    noise = jnp.where(rows == lanes, jnp.broadcast_to(vec[0], (128, 128)), 0.0)
    s_all = s_fin[...].reshape(128, 128) + noise
    total(g_col, 7, gc_send, gc_recv).wait_recv()
    g_c = jnp.transpose(g_col[...].reshape(128, 128))
    inverse = spd_inverse([s_all[i * PIVOTS : (i + 1) * PIVOTS] for i in range(M // PIVOTS)], PIVOTS)

    total(m_all, 3, ma_send, ma_recv).wait_recv()
    mean = tree_sum([m_all[i] for i in range(4)])
    vectors_ref[0] = jnp.broadcast_to(vec[2] - mean, (8, 128))
    vectors_ref[1] = jnp.broadcast_to(vec[1], (8, 128))

    solved_ref[...] = mm(inverse, g_c)

    share.wait_recv()

    @pl.when(owner)
    def _():
        total(s_rs, 15, s_send, s_recv).wait_send()
        total(z_rs, 7, z_send, z_recv).wait_send()
        total(s_rs, 31, f_send, f_recv).wait_send()

    @pl.when(jnp.logical_not(owner))
    def _():
        total(s_rs, 16, s_send, s_recv).wait_send()

    total(m_rs, 7, m_send, m_recv).wait_send()
    total(m_all, 3, ma_send, ma_recv).wait_send()
    total(g_rs, 7, gs_send, gs_recv).wait_send()
    total(g_col, 7, gc_send, gc_recv).wait_send()
    share.wait_send()

    @pl.when(z == r)
    def _():
        total(g_row, 15, gr_send, gr_recv).wait_send()

    @pl.when(z != r)
    def _():
        total(g_row, 16, gr_send, gr_recv).wait_send()


def finish(solved_ref, vectors_ref, pv, g_row, ana_hbm, post_hbm, ana, post, sem):
    solved = solved_ref[...]
    copies = []
    for j in range(4):
        first = (j % 2) * 16 + (j // 2) * 8
        g_j = g_row[first : first + 8].reshape(128, 128)
        here = slice(j * 128, (j + 1) * 128)
        if j == 0:
            both = mm(jnp.concatenate([vectors_ref[0], g_j], 0), solved)
            change = both[8:, :]
            ana[...] = (vectors_ref[1] + both[:8, :])[0:1, :]
            copies.append(pltpu.make_async_copy(ana, ana_hbm, sem.at[4]))
            copies[-1].start()
        else:
            change = mm(g_j, solved)
        post[here, :] = pv[here, :] - change
        copies.append(pltpu.make_async_copy(post.at[here], post_hbm.at[here], sem.at[j]))
        copies[-1].start()
    for copy in copies:
        copy.wait()


def on_device(prior_cov, kern, offsets, obs_noise, background, observed):
    vmem = pl.BlockSpec(memory_space=pltpu.VMEM)
    hbm = pl.BlockSpec(memory_space=pltpu.HBM)
    dma = pltpu.SemaphoreType.DMA

    def tiles(count, rows=8):
        return pltpu.VMEM((count, rows, 128), F32)

    def array(*shape):
        return jax.ShapeDtypeStruct(shape, F32)

    operands = [
        pltpu.with_memory_space_constraint(x, pltpu.HBM)
        for x in (
            prior_cov,
            kern,
            offsets,
            obs_noise.reshape(1, 128),
            background.reshape(1, 128),
            observed.reshape(1, 128),
        )
    ]
    solved, vectors, prior_copy, pieces = pl.pallas_call(
        kernel,
        name="analysis",
        out_shape=(array(128, 128), array(2, 8, 128), array(512, 128), array(32, 16, 128)),
        in_specs=[hbm] * 6,
        out_specs=(vmem,) * 4,
        scratch_shapes=[
            pltpu.SMEM((128,), jnp.int32),
            tiles(3, 1),
            tiles(CHUNKS, GAP),
            tiles(CHUNKS, GAP),
            pltpu.VMEM((8 * STRIDE, 128), F32),
            tiles(16), tiles(32), tiles(2), tiles(8), tiles(16),
            tiles(2, 1), tiles(8, 1), tiles(4, 1),
            tiles(8, 16), tiles(8, 16), tiles(1, 16), tiles(8, 16),
            dma((6,)),
            dma((M // GROUP,)),
            pltpu.SemaphoreType.REGULAR,
        ]
        + [dma] * 18,
        compiler_params=pltpu.CompilerParams(
            collective_id=0, has_side_effects=True, vmem_limit_bytes=40 * 1024 * 1024
        ),
    )(*operands)
    ana, post = pl.pallas_call(
        finish,
        name="finish",
        out_shape=(array(1, 128), array(512, 128)),
        in_specs=[vmem] * 4,
        out_specs=(hbm, hbm),
        scratch_shapes=[
            pltpu.VMEM((1, 128), F32), pltpu.VMEM((512, 128), F32), dma((5,)),
        ],
        compiler_params=pltpu.CompilerParams(vmem_limit_bytes=40 * 1024 * 1024),
    )(solved, vectors, prior_copy, pieces)
    return ana.reshape(128), post


def solution(mesh):
    placed = (P("row", "col"), P(), P(), P(), P("col"), P())
    return jax.shard_map(
        on_device,
        mesh=mesh,
        in_specs=placed,
        out_specs=(P("col"), P("row", "col")),
        check_vma=False,
    )
```
